256 devices in a mesh: lat: 8 (over x, core), lon: 32 (over z, y).
Axes of the slice: x: 4, y: 4, z: 8, core: 2. Of those that a mesh axis runs over, the one named last changes fastest.
Arguments:
- features: bfloat16 [256, 512, 768], P('lat', 'lon'), may hold values from -6 to 6
- cotangent: bfloat16 [256, 512, 768], P('lat', 'lon'), may hold values from -6 to 6
- weight_first: bfloat16 [2, 8, 96, 96], replicated, may hold values from -1 to 1
- weight_second: bfloat16 [2, 8, 96, 96], replicated, may hold values from -1 to 1
Outputs:
- mixed_field: bfloat16 [256, 512, 768], P('lat', 'lon')
- feature_grad: bfloat16 [256, 512, 768], P('lat', 'lon')
- grad_first: float32 [2, 8, 96, 96], replicated
- grad_second: float32 [2, 8, 96, 96], replicated
The draws below stay inside these ranges and needn't reach their ends.
All inputs are finite; a program needn't handle non-finite values.
Results may differ from the reference program's by a relative error of at most 0.012.
The reference program's roundings to bfloat16 on the way count: a program that leaves them out, or rounds other values in their place, can miss the bound.
Values may be sent and summed in bfloat16 or wider, within the bound.
A program may use at most 64 MiB of HBM per device.

```python
import math
import jax
import jax.numpy as jnp
from jax import lax

NB = 8
BS = 96
C = 768
HR = 32
H = 256
W = 512
KW = 256
N_LAT = 8


def draw_weight_first(key, part):
    sample = jax.random.normal(key, (2, NB, BS, BS), jnp.float32)
    column_norm = jnp.sqrt(jnp.sum(sample * sample, axis=(0, 2), keepdims=True))
    return (sample / column_norm).astype(jnp.bfloat16)


def draw_weight_second(key, part):
    sample = jnp.clip(jax.random.normal(key, (2, NB, BS, BS), jnp.float32), -6.0, 6.0)
    return ((sample - jnp.roll(sample, 1, axis=2)) / math.sqrt(4.0 * BS)).astype(jnp.bfloat16)


def shard_levels(own_key, dims, shards, least, largest):
    gain, own = 1.0, jax.random.fold_in(own_key, 6)
    for dim, shards_of in shards:
        steps = jnp.exp(jax.random.uniform(jax.random.fold_in(own, dim), (shards_of,), jnp.float32, least / len(shards), largest / len(shards)))
        gain = gain * jnp.repeat(steps, dims[dim] // shards_of).reshape([-1 if axis == dim else 1 for axis in range(len(dims))])
    return gain


def noise(stream_key, extent, width, reach, cuts=(), kind=jnp.bfloat16):
    level = shard_levels(stream_key, extent, cuts, -0.22, 0.18) if cuts else 1.0
    array = jax.random.normal(stream_key, extent, jnp.float32) * width * level
    return jnp.minimum(jnp.maximum(array, -reach), reach).astype(kind)


def setup_inputs(seed: int = 0) -> dict:
    key_list = jax.random.split(jax.random.key(seed), 5)
    return {
        "features": noise(key_list[0], (H, W, C), 1.0, 6.0, ((0, 8), (1, 32))),
        "cotangent": noise(key_list[1], (H, W, C), 1.0, 6.0, ((0, 8), (1, 32))),
        "weight_first": draw_weight_first(jax.random.fold_in(key_list[4], 71), 0),
        "weight_second": draw_weight_second(jax.random.fold_in(key_list[4], 71), 0),
    }


shrink_level = 0.01
gelu_coeff = 0.7978845608028654

def wave_table(first, second, length):
    product = first[:, None] * second[None, :] % length
    angle = 2.0 * math.pi / length * product.astype(jnp.float32)
    return (jnp.cos(angle) / math.sqrt(length), jnp.sin(angle) / math.sqrt(length))

def batch_product(left, weights):
    return jnp.einsum('mbi,bio->mbo', left.astype(jnp.float32), weights.astype(jnp.float32))

def batch_back(left, weights):
    return jnp.einsum('mbo,bio->mbi', left.astype(jnp.float32), weights.astype(jnp.float32))

def batch_outer(left, right):
    return jnp.einsum('mbi,mbo->bio', left.astype(jnp.float32), right.astype(jnp.float32))

def gelu_parts(values):
    squared = values * values
    tangent = jnp.tanh(gelu_coeff * (values + 0.044715 * squared * values))
    result = 0.5 * values * (1.0 + tangent)
    slope = 0.5 * (1.0 + tangent) + 0.5 * values * (1.0 - tangent * tangent) * gelu_coeff * (1.0 + 3.0 * 0.044715 * squared)
    return (result, slope)

def shrink_parts(values):
    ratio = jnp.tanh(values / shrink_level)
    return (values - shrink_level * ratio, ratio * ratio)

def spectral_block(real_in, imag_in, real_cot, imag_cot, mode_weight, weight_first, weight_second):
    first_re, first_im = (weight_first[0], weight_first[1])
    second_re, second_im = (weight_second[0], weight_second[1])
    pre_real = batch_product(real_in, first_re) - batch_product(imag_in, first_im)
    pre_imag = batch_product(real_in, first_im) + batch_product(imag_in, first_re)
    act_real, slope_real = gelu_parts(pre_real)
    act_imag, slope_imag = gelu_parts(pre_imag)
    hidden_real = act_real.astype(jnp.bfloat16)
    hidden_imag = act_imag.astype(jnp.bfloat16)
    post_real = batch_product(hidden_real, second_re) - batch_product(hidden_imag, second_im)
    post_imag = batch_product(hidden_real, second_im) + batch_product(hidden_imag, second_re)
    shr_real, pass_real = shrink_parts(post_real)
    shr_imag, pass_imag = shrink_parts(post_imag)
    out_real = shr_real.astype(jnp.bfloat16)
    out_imag = shr_imag.astype(jnp.bfloat16)
    grad_post_real = (mode_weight * real_cot.astype(jnp.float32) * pass_real).astype(jnp.bfloat16)
    grad_post_imag = (mode_weight * imag_cot.astype(jnp.float32) * pass_imag).astype(jnp.bfloat16)
    grad_hid_real = batch_back(grad_post_real, second_re) + batch_back(grad_post_imag, second_im)
    grad_hid_imag = batch_back(grad_post_imag, second_re) - batch_back(grad_post_real, second_im)
    grad_pre_real = (grad_hid_real * slope_real).astype(jnp.bfloat16)
    grad_pre_imag = (grad_hid_imag * slope_imag).astype(jnp.bfloat16)
    back_real = (batch_back(grad_pre_real, first_re) + batch_back(grad_pre_imag, first_im)).astype(jnp.bfloat16)
    back_imag = (batch_back(grad_pre_imag, first_re) - batch_back(grad_pre_real, first_im)).astype(jnp.bfloat16)
    grad_second = jnp.stack([batch_outer(hidden_real, grad_post_real) + batch_outer(hidden_imag, grad_post_imag), batch_outer(hidden_real, grad_post_imag) - batch_outer(hidden_imag, grad_post_real)])
    grad_first = jnp.stack([batch_outer(real_in, grad_pre_real) + batch_outer(imag_in, grad_pre_imag), batch_outer(real_in, grad_pre_imag) - batch_outer(imag_in, grad_pre_real)])
    return (out_real, out_imag, back_real, back_imag, grad_first, grad_second)

def lat_forward(coeffs, slab):
    rows_total = slab.shape[0]
    product = jnp.einsum('ah,hrkc->arkc', coeffs.astype(jnp.float32), slab.astype(jnp.float32))
    upper = product[:rows_total]
    lower = product[rows_total:]
    real_part = (upper[:, 0] + lower[:, 1]).astype(jnp.bfloat16)
    imag_part = (upper[:, 1] - lower[:, 0]).astype(jnp.bfloat16)
    return (real_part, imag_part)

def lat_inverse(coeffs, real_part, imag_part):
    rows_total = real_part.shape[0]
    slab = jnp.stack([real_part, imag_part], axis=1)
    product = jnp.einsum('ak,krbc->arbc', coeffs.astype(jnp.float32), slab.astype(jnp.float32))
    upper = product[:rows_total]
    lower = product[rows_total:]
    return jnp.stack([upper[:, 0] - lower[:, 1], lower[:, 0] + upper[:, 1]], axis=1).astype(jnp.bfloat16)

def reference(features, cotangent, weight_first, weight_second):
    kept_block = KW // 16
    lon_cos, lon_sin = wave_table(jnp.arange(KW, dtype=jnp.int32), jnp.arange(W, dtype=jnp.int32), W)
    lon_coeffs = jnp.concatenate([lon_cos, lon_sin]).astype(jnp.bfloat16)

    def lon_forward(band):
        product = jnp.einsum('aw,rwc->rac', lon_coeffs.astype(jnp.float32), band.astype(jnp.float32))
        return jnp.stack([product[:, :KW], -product[:, KW:]], axis=1).astype(jnp.bfloat16)
    spec_field = lax.map(lon_forward, features.reshape(N_LAT, HR, W, C)).reshape(H, 2, KW, C)
    spec_cot = lax.map(lon_forward, cotangent.reshape(N_LAT, HR, W, C)).reshape(H, 2, KW, C)
    lat_cos, lat_sin = wave_table(jnp.arange(H, dtype=jnp.int32), jnp.arange(H, dtype=jnp.int32), H)
    lat_coeffs = jnp.concatenate([lat_cos, lat_sin]).astype(jnp.bfloat16)
    doubled = jnp.where(jnp.arange(KW, dtype=jnp.int32) == 0, 1.0, 2.0).astype(jnp.float32)

    def step(totals, position):
        start = (position * kept_block).astype(jnp.int32)
        field_slab = lax.dynamic_slice_in_dim(spec_field, start, kept_block, 2)
        cot_slab = lax.dynamic_slice_in_dim(spec_cot, start, kept_block, 2)
        real_in, imag_in = lat_forward(lat_coeffs, field_slab)
        real_cot, imag_cot = lat_forward(lat_coeffs, cot_slab)
        modes = H * kept_block
        weight_slab = lax.dynamic_slice_in_dim(doubled, start, kept_block, 0)
        mode_weight = jnp.broadcast_to(weight_slab[None, :], (H, kept_block)).reshape(modes, 1, 1)
        results = spectral_block(real_in.reshape(modes, NB, BS), imag_in.reshape(modes, NB, BS), real_cot.reshape(modes, NB, BS), imag_cot.reshape(modes, NB, BS), mode_weight, weight_first, weight_second)
        out_real, out_imag, back_real, back_imag, grad_first, grad_second = results
        inv_out = lat_inverse(lat_coeffs, out_real.reshape(H, kept_block, C), out_imag.reshape(H, kept_block, C))
        inv_back = lat_inverse(lat_coeffs, back_real.reshape(H, kept_block, C), back_imag.reshape(H, kept_block, C))
        return ((totals[0] + grad_first, totals[1] + grad_second), (inv_out, inv_back))
    zeros_grad = jnp.zeros((2, NB, BS, BS), jnp.float32)
    totals, stacked = lax.scan(step, (zeros_grad, zeros_grad), jnp.arange(16, dtype=jnp.int32))
    inv_out, inv_back = stacked

    def regroup(blocks):
        return jnp.moveaxis(blocks, 0, 2).reshape(N_LAT, HR, 2 * KW, C)
    plain = jnp.concatenate([lon_cos, -lon_sin]).astype(jnp.bfloat16)
    scaled = (plain.astype(jnp.float32) * jnp.concatenate([doubled, doubled])[:, None]).astype(jnp.bfloat16)

    def lon_inverse(coeffs):

        def apply_rows(band):
            return jnp.einsum('aw,rac->rwc', coeffs.astype(jnp.float32), band.astype(jnp.float32)).astype(jnp.bfloat16)
        return apply_rows
    filtered = lax.map(lon_inverse(scaled), regroup(inv_out)).reshape(H, W, C)
    backward = lax.map(lon_inverse(plain), regroup(inv_back)).reshape(H, W, C)
    mixed_field = (features.astype(jnp.float32) + filtered.astype(jnp.float32)).astype(jnp.bfloat16)
    feature_grad = (cotangent.astype(jnp.float32) + backward.astype(jnp.float32)).astype(jnp.bfloat16)
    factor = 1.0 / math.sqrt(H * KW)
    return (mixed_field, feature_grad, totals[0] * factor, totals[1] * factor)
```

```python
import math

import jax
import jax.numpy as jnp
import ml_dtypes
import numpy as np
from jax import lax
from jax.experimental import pallas as pl
from jax.experimental.pallas import tpu as pltpu
from jax.sharding import Mesh
from jax.sharding import PartitionSpec as P

NB = 8
BS = 96
BP = 128
NL, NZ, NY = 8, 8, 4
RB = 8
KB = 8
WB = 16
W = 512
H = 256
KW = 256
CB = RB * BS
NP = 32
SHRINK = 0.01
GELU = 0.7978845608028654
MESH = pl.DeviceIdType.MESH
F32 = jnp.float32
BF16 = jnp.bfloat16


def wave_table(first, second, length):
    product = (first[:, None] * second[None, :]) % length
    angle = np.float32(2.0 * math.pi / length) * product.astype(np.float32)
    root = np.float32(math.sqrt(length))
    return (
        (np.cos(angle) / root).astype(ml_dtypes.bfloat16).astype(np.float32),
        (np.sin(angle) / root).astype(ml_dtypes.bfloat16).astype(np.float32),
    )


def tables():
    lon_cos, lon_sin = wave_table(np.arange(KW), np.arange(W), W)
    lon = np.stack([lon_cos.reshape(NP, KB, W), -lon_sin.reshape(NP, KB, W)], axis=1)
    lon = lon.reshape(2 * KW, W)
    doubled = np.full((NP, 2, KB), 2.0, np.float32)
    doubled[0, :, 0] = 1.0
    plain = lon.T
    scaled = plain * doubled.reshape(1, 2 * KW)
    lat_cos, lat_sin = wave_table(np.arange(H), np.arange(H), H)
    cos = lat_cos.reshape(H, NP, RB)
    sin = lat_sin.reshape(H, NP, RB)
    top = np.stack([cos, sin], axis=2)
    low = np.stack([-sin, cos], axis=2)
    lat = np.concatenate([top, low]).reshape(2 * H, 2 * H)
    return [t.astype(ml_dtypes.bfloat16) for t in (lon, lat, lat.T, scaled, plain)]


def dot(a, b):
    return jnp.dot(a, b, preferred_element_type=F32)


def dot_tb(a, b):
    return lax.dot_general(a, b, (((1,), (1,)), ((), ())), preferred_element_type=F32)


def dot_ta(a, b):
    return lax.dot_general(a, b, (((0,), (0,)), ((), ())), preferred_element_type=F32)


def step_of(index, size):
    half = (index + 1) // 2
    return lax.rem(half + (1 - lax.rem(index, 2)) * (size - 2 * half), size)


def kernel(
    feat, cot, wf, ws, t_lon, t_lat, t_inv, t_scaled, t_plain,
    mixed, fgrad, g_first, g_second,
    buf_a, buf_x, buf_t, buf_b, buf_r, buf_s, buf_o, buf_h, buf_slope, buf_pass,
    buf_d, buf_z, buf_e, buf_u, w1, w2, send_sem, recv_sem,
):
    lat = lax.axis_index("lat")
    zed = lax.axis_index("z")
    why = lax.axis_index("y")
    lon_me = zed * NY + why
    lat_me = lat * NY + why

    barrier = pltpu.get_barrier_semaphore()

    def greet_z(i, carry):
        z = lax.rem(zed + i // NY, NZ)
        y = lax.rem(why + lax.rem(i, NY), NY)
        pl.semaphore_signal(barrier, inc=1, device_id=(lat, z, y), device_id_type=MESH)
        return carry

    def greet_l(i, carry):
        other = lax.rem(lat + i // NY, NL)
        y = lax.rem(why + lax.rem(i, NY), NY)
        pl.semaphore_signal(barrier, inc=1, device_id=(other, zed, y), device_id_type=MESH)
        return carry

    lax.fori_loop(1, NP, greet_z, 0)
    lax.fori_loop(NY, NP, greet_l, 0)

    def exchange(phase, s, src, dst, over_z):
        me = lon_me if over_z else lat_me
        send = send_sem.at[phase, s]
        recv = recv_sem.at[phase, s]

        def one(i, carry):
            step = step_of(i // NY, 8)
            y = lax.rem(why + lax.rem(i, NY), NY)
            if over_z:
                major = lax.rem(zed + step, NZ)
                target = (lat, major, y)
            else:
                major = lax.rem(lat + step, NL)
                target = (major, zed, y)
            pltpu.make_async_remote_copy(
                src_ref=src.at[s, major * NY + y],
                dst_ref=dst.at[s, me],
                send_sem=send,
                recv_sem=recv,
                device_id=target,
                device_id_type=MESH,
            ).start()
            return carry

        lax.fori_loop(1, NP, one, 0)
        pltpu.make_async_copy(src.at[s, me], dst.at[s, me], recv).start()

    def arrived(phase, s, dst):
        pltpu.make_async_copy(dst.at[s], dst.at[s], recv_sem.at[phase, s]).wait()

    def left(phase, s, src):
        part = src.at[s, pl.ds(0, NP - 1)]
        pltpu.make_async_copy(part, part, send_sem.at[phase, s]).wait()

    def pack(s, source):
        def body(y, carry):
            rows = [source[y * RB + r] for r in range(RB)]
            for z in range(NZ):
                pieces = [row[:, z * BS : (z + 1) * BS] for row in rows]
                buf_a[s, z * NY + y] = jnp.concatenate(pieces, axis=1)
            return carry

        lax.fori_loop(0, NY, body, 0)

    def widen(pair):
        zero = jnp.zeros((pair.shape[0], BP - BS), pair.dtype)
        return jnp.concatenate([pair[:, :BS], zero, pair[:, BS:], zero], axis=1)

    def swap_out(s, dst):
        def body(d, carry):
            pieces = []
            for j in range(8):
                low = buf_t[pl.ds(d * 128 + j, 8, stride=8), :]
                high = buf_t[pl.ds(d * 128 + 64 + j, 8, stride=8), :]
                both = jnp.concatenate([low, high], axis=0).astype(BF16)
                pieces.append(both[:, :BS])
            dst[s, d] = jnp.concatenate(pieces, axis=1)
            return carry

        lax.fori_loop(0, NP, body, 0)

    def to_t(out, j):
        view = buf_t.reshape(64, 8, 8, BP)
        view[:, 2 * j] = out[:, :BP].reshape(64, 8, BP)
        view[:, 2 * j + 1] = out[:, BP:].reshape(64, 8, BP)

    def lon_forward(s):
        for j in range(4):
            pair = buf_x[s, :, :, 2 * BS * j : 2 * BS * (j + 1)].reshape(W, 2 * BS)
            to_t(dot(t_lon[...], widen(pair)), j)
        swap_out(s, buf_b)

    def lat_forward(s):
        for j in range(4):
            pair = buf_r[s, :, :, 2 * BS * j : 2 * BS * (j + 1)].reshape(2 * H, 2 * BS)
            out = dot(t_lat[...], widen(pair)).astype(BF16)
            buf_s[s, :, 2 * BP * j : 2 * BP * (j + 1)] = out

    def lat_inverse(s):
        for j in range(4):
            to_t(dot(t_inv[...], buf_o[s, :, 2 * BP * j : 2 * BP * (j + 1)]), j)
        swap_out(s, buf_d)

    def lon_inverse(s):
        table = t_plain if s else t_scaled
        for j in range(3):
            part = buf_z[s, :, :, 2 * BP * j : 2 * BP * (j + 1)].reshape(2 * KW, 2 * BP)
            out = dot(table[...], part).astype(BF16)
            buf_e[s, :, :, 2 * BP * j : 2 * BP * (j + 1)] = out.reshape(NP, WB, 2 * BP)

    def modes(s, k):
        lanes = pl.ds(pl.multiple_of(k * BP, BP), BP)
        return jnp.concatenate([buf_s[s, :H, lanes], buf_s[s, H:, lanes]], axis=1)

    def put_modes(s, k, value):
        lanes = pl.ds(pl.multiple_of(k * BP, BP), BP)
        buf_o[s, :H, lanes] = value[:, :BP]
        buf_o[s, H:, lanes] = value[:, BP:]

    def mlp_forward(k, carry):
        pre = dot(modes(0, k), w1[...])
        squared = pre * pre
        tangent = jnp.tanh(GELU * (pre + 0.044715 * squared * pre))
        hidden = (0.5 * pre * (1.0 + tangent)).astype(BF16)
        buf_h[k] = hidden
        buf_slope[k] = 0.5 * (1.0 + tangent) + 0.5 * pre * (1.0 - tangent * tangent) * GELU * (
            1.0 + 3.0 * 0.044715 * squared
        )
        post = dot(hidden, w2[...])
        ratio = jnp.tanh(post / SHRINK)
        put_modes(0, k, (post - SHRINK * ratio).astype(BF16))
        weight = jnp.where(lat_me * KB + k == 0, 1.0, 2.0).astype(F32)
        buf_pass[k] = weight * (ratio * ratio)
        return carry

    g_first[...] = jnp.zeros_like(g_first)
    g_second[...] = jnp.zeros_like(g_second)

    def mlp_backward(k, carry):
        d_post = (modes(1, k).astype(F32) * buf_pass[k]).astype(BF16)
        d_pre = (dot_tb(d_post, w2[...]) * buf_slope[k]).astype(BF16)
        put_modes(1, k, dot_tb(d_pre, w1[...]).astype(BF16))
        g_second[...] += dot_ta(buf_h[k], d_post)
        g_first[...] += dot_ta(modes(0, k), d_pre)
        return carry

    def unpack(s, source, target):
        def body(y, carry):
            blocks = [buf_u[s, z * NY + y] for z in range(NZ)]
            for r in range(RB):
                pieces = [block[:, r * BS : (r + 1) * BS] for block in blocks]
                row = jnp.concatenate(pieces, axis=1).astype(F32)
                target[y * RB + r] = (source[y * RB + r].astype(F32) + row).astype(BF16)
            return carry

        lax.fori_loop(0, NY, body, 0)

    pack(0, feat)
    pl.semaphore_wait(barrier, 2 * NP - NY - 1)
    exchange(0, 0, buf_a, buf_x, True)
    pack(1, cot)
    exchange(0, 1, buf_a, buf_x, True)

    for source, target in ((wf, w1), (ws, w2)):
        target[...] = jnp.zeros_like(target)
        real = source[0, zed]
        imag = source[1, zed]
        target[0:BS, 0:BS] = real
        target[0:BS, BP : BP + BS] = imag
        target[BP : BP + BS, 0:BS] = -imag
        target[BP : BP + BS, BP : BP + BS] = real

    arrived(0, 0, buf_x)
    lon_forward(0)
    exchange(1, 0, buf_b, buf_r, False)
    arrived(1, 0, buf_r)
    lat_forward(0)
    lax.fori_loop(0, KB, mlp_forward, 0)
    lat_inverse(0)
    exchange(2, 0, buf_d, buf_z, False)
    arrived(0, 1, buf_x)
    lon_forward(1)
    exchange(1, 1, buf_b, buf_r, False)
    arrived(2, 0, buf_z)
    lon_inverse(0)
    exchange(3, 0, buf_e, buf_u, True)
    arrived(1, 1, buf_r)
    lat_forward(1)
    lax.fori_loop(0, KB, mlp_backward, 0)
    lat_inverse(1)
    exchange(2, 1, buf_d, buf_z, False)
    arrived(2, 1, buf_z)
    lon_inverse(1)
    exchange(3, 1, buf_e, buf_u, True)
    arrived(3, 0, buf_u)
    unpack(0, feat, mixed)
    arrived(3, 1, buf_u)
    unpack(1, cot, fgrad)
    for s in range(2):
        left(0, s, buf_a)
        left(1, s, buf_b)
        left(2, s, buf_d)
        left(3, s, buf_e)


def fold(total):
    real = total[:BS, :BS] + total[BP : BP + BS, BP : BP + BS]
    imag = total[:BS, BP : BP + BS] - total[BP : BP + BS, :BS]
    return jnp.stack([real, imag])


def shards(features, cotangent, weight_first, weight_second):
    vmem = pl.BlockSpec(memory_space=pltpu.VMEM)
    chunks = (2, NP, 16, CB)
    grads = jax.ShapeDtypeStruct((2 * BP, 2 * BP), F32)
    rows = jax.ShapeDtypeStruct(features.shape, BF16)
    mixed, fgrad, g_first, g_second = pl.pallas_call(
        kernel,
        out_shape=(rows, rows, grads, grads),
        in_specs=[vmem] * 9,
        out_specs=[vmem] * 4,
        scratch_shapes=[
            pltpu.VMEM(chunks, BF16),
            pltpu.VMEM(chunks, BF16),
            pltpu.VMEM((4096, BP), F32),
            pltpu.VMEM(chunks, BF16),
            pltpu.VMEM(chunks, BF16),
            pltpu.VMEM((2, 2 * H, KB * BP), BF16),
            pltpu.VMEM((2, 2 * H, KB * BP), BF16),
            pltpu.VMEM((KB, 2 * BP, 2 * BP), BF16),
            pltpu.VMEM((KB, 2 * BP, 2 * BP), F32),
            pltpu.VMEM((KB, 2 * BP, 2 * BP), F32),
            pltpu.VMEM(chunks, BF16),
            pltpu.VMEM(chunks, BF16),
            pltpu.VMEM(chunks, BF16),
            pltpu.VMEM(chunks, BF16),
            pltpu.VMEM((2 * BP, 2 * BP), BF16),
            pltpu.VMEM((2 * BP, 2 * BP), BF16),
            pltpu.SemaphoreType.DMA((4, 2)),
            pltpu.SemaphoreType.DMA((4, 2)),
        ],
        compiler_params=pltpu.CompilerParams(
            collective_id=0, has_side_effects=True, vmem_limit_bytes=48 << 20
        ),
    )(features, cotangent, weight_first, weight_second, *[jnp.asarray(t) for t in tables()])
    summed = lax.psum(jnp.stack([fold(g_first), fold(g_second)]), ("lat", "y"))
    gathered = lax.all_gather(summed, "z", axis=2)
    factor = 1.0 / math.sqrt(H * KW)
    return (mixed, fgrad, gathered[0] * factor, gathered[1] * factor)


def solution(mesh):
    split = Mesh(mesh.devices.reshape(NL, NZ, NY), ("lat", "z", "y"))
    spec = P("lat", ("z", "y"), None)
    return jax.shard_map(
        shards,
        mesh=split,
        in_specs=(spec, spec, P(), P()),
        out_specs=(spec, spec, P(), P()),
        check_vma=False,
    )
```

```python
import math

import jax
import jax.numpy as jnp
import ml_dtypes
import numpy as np
from jax import lax
from jax.experimental import pallas as pl
from jax.experimental.pallas import tpu as pltpu
from jax.sharding import Mesh
from jax.sharding import PartitionSpec as P

NB = 8
BS = 96
BP = 128
NL, NZ, NY = 8, 8, 4
RB = 8
KB = 8
WB = 16
W = 512
H = 256
KW = 256
CB = RB * BS
NP = 32
GR = 48
SHRINK = 0.01
GELU = 0.7978845608028654
MESH = pl.DeviceIdType.MESH
F32 = jnp.float32
BF16 = jnp.bfloat16


def wave_table(first, second, length):
    product = (first[:, None] * second[None, :]) % length
    angle = np.float32(2.0 * math.pi / length) * product.astype(np.float32)
    root = np.float32(math.sqrt(length))
    return (
        (np.cos(angle) / root).astype(ml_dtypes.bfloat16).astype(np.float32),
        (np.sin(angle) / root).astype(ml_dtypes.bfloat16).astype(np.float32),
    )


def tables():
    lon_cos, lon_sin = wave_table(np.arange(KW), np.arange(W), W)
    lon = np.stack([lon_cos.reshape(NP, KB, W), -lon_sin.reshape(NP, KB, W)], axis=1)
    lon = lon.reshape(2 * KW, W)
    doubled = np.full((NP, 2, KB), 2.0, np.float32)
    doubled[0, :, 0] = 1.0
    plain = lon.T
    scaled = plain * doubled.reshape(1, 2 * KW)
    lat_cos, lat_sin = wave_table(np.arange(H), np.arange(H), H)
    cos = lat_cos.reshape(H, NP, RB)
    sin = lat_sin.reshape(H, NP, RB)
    top = np.stack([cos, sin], axis=2)
    low = np.stack([-sin, cos], axis=2)
    lat = np.concatenate([top, low]).reshape(2 * H, 2 * H)
    return [t.astype(ml_dtypes.bfloat16) for t in (lon, lat, lat.T, scaled, plain)]


def dot(a, b):
    return jnp.dot(a, b, preferred_element_type=F32)


def dot_tb(a, b):
    return lax.dot_general(a, b, (((1,), (1,)), ((), ())), preferred_element_type=F32)


def dot_ta(a, b):
    return lax.dot_general(a, b, (((0,), (0,)), ((), ())), preferred_element_type=F32)


def step_of(index, size):
    half = (index + 1) // 2
    return lax.rem(half + (1 - lax.rem(index, 2)) * (size - 2 * half), size)


def kernel(
    feat_hbm, cot_hbm, wf, ws, h_lon, h_lat, h_inv, h_scaled, h_plain,
    mixed, fgrad, out_first, out_second,
    feat, cot, t_lon, t_lat, t_inv, t_scaled, t_plain, g_first, g_second,
    buf_a, buf_x, buf_t, buf_b, buf_r, buf_s, buf_o, buf_h, buf_slope, buf_pass,
    buf_d, buf_z, buf_e, buf_u, w1, w2, send_sem, recv_sem,
    part_g, part_l, part_p, part_y, part_q, part_z, part_c, g_send, g_recv, load_sem,
):
    lat = lax.axis_index("lat")
    zed = lax.axis_index("z")
    why = lax.axis_index("y")
    lon_me = zed * NY + why
    lat_me = lat * NY + why

    loads = [
        pltpu.make_async_copy(source, target, load_sem.at[i])
        for i, (source, target) in enumerate(
            [
                (feat_hbm, feat), (cot_hbm, cot), (h_lon, t_lon), (h_lat, t_lat),
                (h_inv, t_inv), (h_scaled, t_scaled), (h_plain, t_plain),
            ]
        )
    ]
    for load in loads:
        load.start()

    barrier = pltpu.get_barrier_semaphore()

    def greet_z(i, carry):
        z = lax.rem(zed + i // NY, NZ)
        y = lax.rem(why + lax.rem(i, NY), NY)
        pl.semaphore_signal(barrier, inc=1, device_id=(lat, z, y), device_id_type=MESH)
        return carry

    def greet_l(i, carry):
        other = lax.rem(lat + i // NY, NL)
        y = lax.rem(why + lax.rem(i, NY), NY)
        pl.semaphore_signal(barrier, inc=1, device_id=(other, zed, y), device_id_type=MESH)
        return carry

    lax.fori_loop(1, NP, greet_z, 0)
    lax.fori_loop(NY, NP, greet_l, 0)

    def exchange(phase, s, src, dst, over_z):
        me = lon_me if over_z else lat_me
        send = send_sem.at[phase, s]
        recv = recv_sem.at[phase, s]

        def one(i, carry):
            step = step_of(i // NY, 8)
            y = lax.rem(why + lax.rem(i, NY), NY)
            if over_z:
                major = lax.rem(zed + step, NZ)
                target = (lat, major, y)
            else:
                major = lax.rem(lat + step, NL)
                target = (major, zed, y)
            pltpu.make_async_remote_copy(
                src_ref=src.at[s, major * NY + y],
                dst_ref=dst.at[s, me],
                send_sem=send,
                recv_sem=recv,
                device_id=target,
                device_id_type=MESH,
            ).start()
            return carry

        lax.fori_loop(1, NP, one, 0)
        pltpu.make_async_copy(src.at[s, me], dst.at[s, me], recv).start()

    def arrived(phase, s, dst):
        pltpu.make_async_copy(dst.at[s], dst.at[s], recv_sem.at[phase, s]).wait()

    def left(phase, s, src):
        part = src.at[s, pl.ds(0, NP - 1)]
        pltpu.make_async_copy(part, part, send_sem.at[phase, s]).wait()

    def pack(s, source):
        def body(y, carry):
            rows = [source[y * RB + r] for r in range(RB)]
            for z in range(NZ):
                pieces = [row[:, z * BS : (z + 1) * BS] for row in rows]
                buf_a[s, z * NY + y] = jnp.concatenate(pieces, axis=1)
            return carry

        lax.fori_loop(0, NY, body, 0)

    def widen(pair):
        zero = jnp.zeros((pair.shape[0], BP - BS), pair.dtype)
        return jnp.concatenate([pair[:, :BS], zero, pair[:, BS:], zero], axis=1)

    def swap_out(s, dst):
        def body(d, carry):
            pieces = []
            for j in range(8):
                low = buf_t[pl.ds(d * 128 + j, 8, stride=8), :]
                high = buf_t[pl.ds(d * 128 + 64 + j, 8, stride=8), :]
                both = jnp.concatenate([low, high], axis=0).astype(BF16)
                pieces.append(both[:, :BS])
            dst[s, d] = jnp.concatenate(pieces, axis=1)
            return carry

        lax.fori_loop(0, NP, body, 0)

    def to_t(out, j):
        view = buf_t.reshape(64, 8, 8, BP)
        view[:, 2 * j] = out[:, :BP].reshape(64, 8, BP)
        view[:, 2 * j + 1] = out[:, BP:].reshape(64, 8, BP)

    def lon_forward(s):
        for j in range(4):
            pair = buf_x[s, :, :, 2 * BS * j : 2 * BS * (j + 1)].reshape(W, 2 * BS)
            to_t(dot(t_lon[...], widen(pair)), j)
        swap_out(s, buf_b)

    def lat_forward(s):
        for j in range(4):
            pair = buf_r[s, :, :, 2 * BS * j : 2 * BS * (j + 1)].reshape(2 * H, 2 * BS)
            out = dot(t_lat[...], widen(pair)).astype(BF16)
            buf_s[s, :, 2 * BP * j : 2 * BP * (j + 1)] = out

    def lat_inverse(s):
        for j in range(4):
            to_t(dot(t_inv[...], buf_o[s, :, 2 * BP * j : 2 * BP * (j + 1)]), j)
        swap_out(s, buf_d)

    def lon_inverse(s):
        table = t_plain if s else t_scaled
        for j in range(3):
            part = buf_z[s, :, :, 2 * BP * j : 2 * BP * (j + 1)].reshape(2 * KW, 2 * BP)
            out = dot(table[...], part).astype(BF16)
            buf_e[s, :, :, 2 * BP * j : 2 * BP * (j + 1)] = out.reshape(NP, WB, 2 * BP)

    def modes(s, k):
        lanes = pl.ds(pl.multiple_of(k * BP, BP), BP)
        return jnp.concatenate([buf_s[s, :H, lanes], buf_s[s, H:, lanes]], axis=1)

    def put_modes(s, k, value):
        lanes = pl.ds(pl.multiple_of(k * BP, BP), BP)
        buf_o[s, :H, lanes] = value[:, :BP]
        buf_o[s, H:, lanes] = value[:, BP:]

    def mlp_forward(k, carry):
        pre = dot(modes(0, k), w1[...])
        squared = pre * pre
        tangent = jnp.tanh(GELU * (pre + 0.044715 * squared * pre))
        hidden = (0.5 * pre * (1.0 + tangent)).astype(BF16)
        buf_h[k] = hidden
        buf_slope[k] = 0.5 * (1.0 + tangent) + 0.5 * pre * (1.0 - tangent * tangent) * GELU * (
            1.0 + 3.0 * 0.044715 * squared
        )
        post = dot(hidden, w2[...])
        ratio = jnp.tanh(post / SHRINK)
        put_modes(0, k, (post - SHRINK * ratio).astype(BF16))
        weight = jnp.where(lat_me * KB + k == 0, 1.0, 2.0).astype(F32)
        buf_pass[k] = weight * (ratio * ratio)
        return carry

    g_first[...] = jnp.zeros_like(g_first)
    g_second[...] = jnp.zeros_like(g_second)

    def mlp_backward(k, carry):
        d_post = (modes(1, k).astype(F32) * buf_pass[k]).astype(BF16)
        d_pre = (dot_tb(d_post, w2[...]) * buf_slope[k]).astype(BF16)
        put_modes(1, k, dot_tb(d_pre, w1[...]).astype(BF16))
        g_second[...] += dot_ta(buf_h[k], d_post)
        g_first[...] += dot_ta(modes(0, k), d_pre)
        return carry

    def unpack(s, source, target):
        def body(y, carry):
            blocks = [buf_u[s, z * NY + y] for z in range(NZ)]
            for r in range(RB):
                pieces = [block[:, r * BS : (r + 1) * BS] for block in blocks]
                row = jnp.concatenate(pieces, axis=1).astype(F32)
                target[y * RB + r] = (source[y * RB + r].astype(F32) + row).astype(BF16)
            return carry

        lax.fori_loop(0, NY, body, 0)

    def fold():
        for which, total in ((0, g_first), (1, g_second)):
            real = total[:BS, :BP] + total[BP : BP + BS, BP:]
            imag = total[:BS, BP:] - total[BP : BP + BS, :BP]
            for ri, plane in ((0, real), (1, imag)):
                part_g[4 * which + 2 * ri] = plane[:GR]
                part_g[4 * which + 2 * ri + 1] = plane[GR:]

    def gather(stage, count, source_of, dst, target_of):
        def one(i, carry):
            source, target = target_of(i)
            pltpu.make_async_remote_copy(
                src_ref=source,
                dst_ref=dst,
                send_sem=g_send.at[stage],
                recv_sem=g_recv.at[stage],
                device_id=target,
                device_id_type=MESH,
            ).start()
            return carry

        lax.fori_loop(1, count, one, 0)
        if source_of is not None:
            pltpu.make_async_copy(source_of, dst, g_recv.at[stage]).start()

    def g_arrived(stage, ref):
        pltpu.make_async_copy(ref, ref, g_recv.at[stage]).wait()

    def g_left(stage, ref):
        pltpu.make_async_copy(ref, ref, g_send.at[stage]).wait()

    row = lat // 2
    core = lax.rem(lat, 2)

    def to_lat(i):
        other = lax.rem(lat + i, NL)
        return part_g.at[other], (other, zed, why)

    def to_y(i):
        return part_p, (lat, zed, lax.rem(why + i, NY))

    def to_z(i):
        return part_q, (lat, lax.rem(zed + i, NZ), why)

    def to_x(i):
        return part_z, (2 * lax.rem(row + i, NL // 2) + core, zed, why)

    def grads_lat():
        fold()
        gather(0, NL, part_g.at[lat], part_l.at[lat], to_lat)

    def grads_y():
        g_arrived(0, part_l)
        total = part_l[0]
        for i in range(1, NL):
            total = total + part_l[i]
        part_p[...] = total
        gather(1, NY, part_p, part_y.at[why], to_y)

    def grads_z():
        g_arrived(1, part_y)
        total = part_y[0]
        for i in range(1, NY):
            total = total + part_y[i]
        part_q[...] = total * (1.0 / math.sqrt(H * KW))
        gather(2, NZ, part_q, part_z.at[zed], to_z)

    def grads_x():
        g_arrived(2, part_z)
        gather(3, NL // 2, part_z, part_c.at[core, row], to_x)

    def mate_copy():
        return pltpu.make_async_remote_copy(
            src_ref=part_c.at[core],
            dst_ref=part_c.at[core],
            send_sem=g_send.at[4],
            recv_sem=g_recv.at[4],
            device_id=(2 * row + 1 - core, zed, why),
            device_id_type=MESH,
        )

    def grads_core():
        g_arrived(3, part_c.at[core])
        mate_copy().start()

    def grads_out():
        g_arrived(4, part_c.at[0])
        for piece in range(NL):
            target = (out_first, out_second)[piece // 4]
            rows = slice((piece % 2) * GR, (piece % 2 + 1) * GR)
            for z in range(NZ):
                target[(piece // 2) % 2, z, rows, :] = part_c[piece % 2, piece // 2, z][:, :BS]
        g_left(0, part_g.at[pl.ds(0, NL - 1)])
        g_left(1, part_y.at[pl.ds(0, NY - 1)])
        g_left(2, part_z.at[pl.ds(0, NZ - 1)])
        g_left(3, part_c.at[0, pl.ds(0, NL // 2 - 1)])
        g_left(4, part_c.at[0])

    loads[0].wait()
    pack(0, feat)
    pl.semaphore_wait(barrier, 2 * NP - NY - 1)
    exchange(0, 0, buf_a, buf_x, True)
    loads[1].wait()
    pack(1, cot)
    exchange(0, 1, buf_a, buf_x, True)

    for source, target in ((wf, w1), (ws, w2)):
        target[...] = jnp.zeros_like(target)
        real = source[0, zed]
        imag = source[1, zed]
        target[0:BS, 0:BS] = real
        target[0:BS, BP : BP + BS] = imag
        target[BP : BP + BS, 0:BS] = -imag
        target[BP : BP + BS, BP : BP + BS] = real
    for load in loads[2:]:
        load.wait()

    arrived(0, 0, buf_x)
    lon_forward(0)
    exchange(1, 0, buf_b, buf_r, False)
    arrived(1, 0, buf_r)
    lat_forward(0)
    lax.fori_loop(0, KB, mlp_forward, 0)
    lat_inverse(0)
    exchange(2, 0, buf_d, buf_z, False)
    arrived(0, 1, buf_x)
    lon_forward(1)
    exchange(1, 1, buf_b, buf_r, False)
    arrived(2, 0, buf_z)
    lon_inverse(0)
    exchange(3, 0, buf_e, buf_u, True)
    arrived(1, 1, buf_r)
    lat_forward(1)
    lax.fori_loop(0, KB, mlp_backward, 0)
    grads_lat()
    lat_inverse(1)
    exchange(2, 1, buf_d, buf_z, False)
    grads_y()
    grads_z()
    arrived(2, 1, buf_z)
    lon_inverse(1)
    exchange(3, 1, buf_e, buf_u, True)
    grads_x()
    arrived(3, 0, buf_u)
    unpack(0, feat, mixed)
    grads_core()
    grads_out()
    arrived(3, 1, buf_u)
    unpack(1, cot, fgrad)
    for s in range(2):
        left(0, s, buf_a)
        left(1, s, buf_b)
        left(2, s, buf_d)
        left(3, s, buf_e)


def shards(features, cotangent, weight_first, weight_second):
    vmem = pl.BlockSpec(memory_space=pltpu.VMEM)
    hbm = pl.BlockSpec(memory_space=pltpu.HBM)
    chunks = (2, NP, 16, CB)
    grads = jax.ShapeDtypeStruct((2, NB, BS, BS), F32)
    rows = jax.ShapeDtypeStruct(features.shape, BF16)
    piece = (GR, BP)
    return pl.pallas_call(
        kernel,
        out_shape=(rows, rows, grads, grads),
        in_specs=[hbm, hbm, vmem, vmem] + [hbm] * 5,
        out_specs=[vmem] * 4,
        scratch_shapes=[
            pltpu.VMEM(features.shape, BF16),
            pltpu.VMEM(features.shape, BF16),
        ]
        + [pltpu.VMEM((512, 512), BF16)] * 5
        + [
            pltpu.VMEM((2 * BP, 2 * BP), F32),
            pltpu.VMEM((2 * BP, 2 * BP), F32),
            pltpu.VMEM(chunks, BF16),
            pltpu.VMEM(chunks, BF16),
            pltpu.VMEM((4096, BP), F32),
            pltpu.VMEM(chunks, BF16),
            pltpu.VMEM(chunks, BF16),
            pltpu.VMEM((2, 2 * H, KB * BP), BF16),
            pltpu.VMEM((2, 2 * H, KB * BP), BF16),
            pltpu.VMEM((KB, 2 * BP, 2 * BP), BF16),
            pltpu.VMEM((KB, 2 * BP, 2 * BP), F32),
            pltpu.VMEM((KB, 2 * BP, 2 * BP), F32),
            pltpu.VMEM(chunks, BF16),
            pltpu.VMEM(chunks, BF16),
            pltpu.VMEM(chunks, BF16),
            pltpu.VMEM(chunks, BF16),
            pltpu.VMEM((2 * BP, 2 * BP), BF16),
            pltpu.VMEM((2 * BP, 2 * BP), BF16),
            pltpu.SemaphoreType.DMA((4, 2)),
            pltpu.SemaphoreType.DMA((4, 2)),
            pltpu.VMEM((NL,) + piece, F32),
            pltpu.VMEM((NL,) + piece, F32),
            pltpu.VMEM(piece, F32),
            pltpu.VMEM((NY,) + piece, F32),
            pltpu.VMEM(piece, F32),
            pltpu.VMEM((NZ,) + piece, F32),
            pltpu.VMEM((2, NL // 2, NZ) + piece, F32),
            pltpu.SemaphoreType.DMA((5,)),
            pltpu.SemaphoreType.DMA((5,)),
            pltpu.SemaphoreType.DMA((7,)),
        ],
        compiler_params=pltpu.CompilerParams(
            collective_id=0, has_side_effects=True, vmem_limit_bytes=58 << 20
        ),
    )(features, cotangent, weight_first, weight_second, *[jnp.asarray(t) for t in tables()])


def solution(mesh):
    split = Mesh(mesh.devices.reshape(NL, NZ, NY), ("lat", "z", "y"))
    spec = P("lat", ("z", "y"), None)
    return jax.shard_map(
        shards,
        mesh=split,
        in_specs=(spec, spec, P(), P()),
        out_specs=(spec, spec, P(), P()),
        check_vma=False,
    )
```

```python
import math

import jax
import jax.numpy as jnp
import ml_dtypes
import numpy as np
from jax import lax
from jax.experimental import pallas as pl
from jax.experimental.pallas import tpu as pltpu
from jax.sharding import Mesh
from jax.sharding import PartitionSpec as P

NB = 8
BS = 96
BP = 128
NL, NZ, NY = 8, 8, 4
RB = 8
KB = 8
WB = 16
W = 512
H = 256
KW = 256
RH = 4
CH = RH * BS
CB = RB * BS
NP = 32
GR = 48
SHRINK = 0.01
GELU = 0.7978845608028654
MESH = pl.DeviceIdType.MESH
F32 = jnp.float32
BF16 = jnp.bfloat16


def wave_table(first, second, length):
    product = (first[:, None] * second[None, :]) % length
    angle = np.float32(2.0 * math.pi / length) * product.astype(np.float32)
    root = np.float32(math.sqrt(length))
    return (
        (np.cos(angle) / root).astype(ml_dtypes.bfloat16).astype(np.float32),
        (np.sin(angle) / root).astype(ml_dtypes.bfloat16).astype(np.float32),
    )


def tables():
    lon_cos, lon_sin = wave_table(np.arange(KW), np.arange(W), W)
    lon = np.stack([lon_cos.reshape(NP, KB, W), -lon_sin.reshape(NP, KB, W)], axis=1)
    lon = lon.reshape(2 * KW, W)
    doubled = np.full((NP, 2, KB), 2.0, np.float32)
    doubled[0, :, 0] = 1.0
    plain = lon.T
    scaled = plain * doubled.reshape(1, 2 * KW)
    lat_cos, lat_sin = wave_table(np.arange(H), np.arange(H), H)
    cos = lat_cos.reshape(H, NP, 2, RH).swapaxes(1, 2)
    sin = lat_sin.reshape(H, NP, 2, RH).swapaxes(1, 2)
    top = np.stack([cos, sin], axis=3)
    low = np.stack([-sin, cos], axis=3)
    lat = np.concatenate([top, low]).reshape(2 * H, 2 * H)
    return np.stack([lon, lat, lat.T, scaled, plain]).astype(ml_dtypes.bfloat16)


def dot(a, b):
    return jnp.dot(a, b, preferred_element_type=F32)


def dot_tb(a, b):
    return lax.dot_general(a, b, (((1,), (1,)), ((), ())), preferred_element_type=F32)


def dot_ta(a, b):
    return lax.dot_general(a, b, (((0,), (0,)), ((), ())), preferred_element_type=F32)


def step_of(index, size):
    half = (index + 1) // 2
    return lax.rem(half + (1 - lax.rem(index, 2)) * (size - 2 * half), size)


def kernel(
    feat_hbm, cot_hbm, wf, ws, h_tables,
    mixed, fgrad, out_first, out_second,
    feat, cot, t_lon, t_lat, t_inv, t_scaled, t_plain, buf_w, g_first, g_second,
    buf_a, buf_x, buf_t, buf_b, buf_r, buf_s, buf_o, buf_h, buf_slope, buf_pass,
    buf_d, buf_z, buf_e, buf_u, w1, w2, send_sem, recv_sem,
    part_g, part_l, part_p, part_y, part_q, part_z, part_c, g_send, g_recv, load_sem,
):
    lat = lax.axis_index("lat")
    zed = lax.axis_index("z")
    why = lax.axis_index("y")
    lon_me = zed * NY + why
    lat_me = lat * NY + why

    loads = [
        pltpu.make_async_copy(source, target, load_sem.at[i])
        for i, (source, target) in enumerate(
            [
                (feat_hbm, feat), (cot_hbm, cot), (h_tables.at[0], t_lon), (h_tables.at[1], t_lat),
                (h_tables.at[2], t_inv), (h_tables.at[3], t_scaled), (h_tables.at[4], t_plain),
            ]
        )
    ]
    for load in loads:
        load.start()

    barrier = pltpu.get_barrier_semaphore()

    def greet_z(i, carry):
        z = lax.rem(zed + i // NY, NZ)
        y = lax.rem(why + lax.rem(i, NY), NY)
        pl.semaphore_signal(barrier, inc=1, device_id=(lat, z, y), device_id_type=MESH)
        return carry

    def greet_l(i, carry):
        other = lax.rem(lat + i // NY, NL)
        y = lax.rem(why + lax.rem(i, NY), NY)
        pl.semaphore_signal(barrier, inc=1, device_id=(other, zed, y), device_id_type=MESH)
        return carry

    lax.fori_loop(1, NP, greet_z, 0)
    lax.fori_loop(NY, NP, greet_l, 0)

    row = lat // 2
    core = lax.rem(lat, 2)

    def send(phase, t, src, dst, over_z, major, y):
        me = lon_me if over_z else lat_me
        to = major * NY + y
        target = (lat, major, y) if over_z else (major, zed, y)

        @pl.when(to != me)
        def _():
            pltpu.make_async_remote_copy(
                src_ref=src.at[t, to],
                dst_ref=dst.at[t, me],
                send_sem=send_sem.at[phase, t],
                recv_sem=recv_sem.at[phase, t],
                device_id=target,
                device_id_type=MESH,
            ).start()

        @pl.when(to == me)
        def _():
            pltpu.make_async_copy(src.at[t, me], dst.at[t, me], recv_sem.at[phase, t]).start()

    def turn(i):
        return lax.rem(why + i, NY)

    def arrived(phase, t, dst):
        pltpu.make_async_copy(dst.at[t], dst.at[t], recv_sem.at[phase, t]).wait()

    def left(phase, t, src):
        part = src.at[t, pl.ds(0, NP - 1)]
        pltpu.make_async_copy(part, part, send_sem.at[phase, t]).wait()

    def pack(t, source):
        def body(y, carry):
            rows = [source[y * RB + (t % 2) * RH + r] for r in range(RH)]
            for z in range(NZ):
                pieces = [r[:, z * BS : (z + 1) * BS] for r in rows]
                buf_a[t, z * NY + y] = jnp.concatenate(pieces, axis=1)
            return carry

        lax.fori_loop(0, NY, body, 0)

    def send_rows(t):
        def body(i, carry):
            z = lax.rem(zed + step_of(i // NY, NZ), NZ)
            send(0, t, buf_a, buf_x, True, z, turn(lax.rem(i, NY)))
            return carry

        lax.fori_loop(0, NP, body, 0)

    def widen(pair):
        zero = jnp.zeros((pair.shape[0], BP - BS), pair.dtype)
        return jnp.concatenate([pair[:, :BS], zero, pair[:, BS:], zero], axis=1)

    def lon_forward(t):
        for j in range(2):
            pair = buf_x[t, :, :, 2 * BS * j : 2 * BS * (j + 1)].reshape(W, 2 * BS)
            buf_w[:, 2 * BP * j : 2 * BP * (j + 1)] = widen(pair)
        view = buf_t.at[pl.ds(0, 512)].reshape(8, 2, RH, KB, BP)

        def chunk(m, carry):
            x = lax.rem(row + step_of(m, NL // 2), NL // 2)
            coeffs = t_lon[pl.ds(pl.multiple_of(x * 128, 128), 128), :]
            for j in range(2):
                out = dot(coeffs, buf_w[:, 2 * BP * j : 2 * BP * (j + 1)])
                view[:, :, 2 * j] = out[:, :BP].reshape(8, 2, KB, BP)
                view[:, :, 2 * j + 1] = out[:, BP:].reshape(8, 2, KB, BP)

            def one(i, inner):
                major = i // NY
                y = turn(lax.rem(i, NY))
                base = (major * NY + y) * 64
                pieces = [
                    buf_t[pl.ds(base + k, 8, stride=8), :].astype(BF16)[:, :BS] for k in range(KB)
                ]
                buf_b[t, 8 * x + major * NY + y] = jnp.concatenate(pieces, axis=1)
                send(1, t, buf_b, buf_r, False, 2 * x + major, y)
                return inner

            return lax.fori_loop(0, 8, one, carry)

        lax.fori_loop(0, NL // 2, chunk, 0)

    def lat_forward(s):
        for j in range(4):
            lanes = slice(2 * BS * j, 2 * BS * (j + 1))
            pair = jnp.concatenate(
                [buf_r[2 * s + h, :, :, lanes].reshape(H, 2 * BS) for h in range(2)], axis=0
            )
            out = dot(t_lat[...], widen(pair)).astype(BF16)
            buf_s[s, :, 2 * BP * j : 2 * BP * (j + 1)] = out

    def lat_inverse(t):
        view = buf_t.reshape(16, KB, 8, BP)

        def chunk(m, carry):
            half = lax.rem(row // 2 + m, 2)
            start = (t % 2) * H + half * 128
            coeffs = t_inv[pl.ds(pl.multiple_of(start, 128), 128), :]
            for j in range(4):
                out = dot(coeffs, buf_o[t // 2, :, 2 * BP * j : 2 * BP * (j + 1)])
                view[:, 2 * j] = out[:, :BP].reshape(16, 8, BP)
                view[:, 2 * j + 1] = out[:, BP:].reshape(16, 8, BP)

            def one(i, inner):
                major = i // NY
                y = turn(lax.rem(i, NY))
                base = (major * NY + y) * 64
                pieces = []
                for r in range(RH):
                    low = buf_t[pl.ds(base + r, 8, stride=8), :]
                    high = buf_t[pl.ds(base + RH + r, 8, stride=8), :]
                    pieces.append(jnp.concatenate([low, high], axis=0).astype(BF16)[:, :BS])
                buf_d[t, 16 * half + major * NY + y] = jnp.concatenate(pieces, axis=1)
                send(2, t, buf_d, buf_z, False, 4 * half + major, y)
                return inner

            return lax.fori_loop(0, 16, one, carry)

        lax.fori_loop(0, 2, chunk, 0)

    def lon_inverse(t):
        table = t_plain if t // 2 else t_scaled

        def chunk(m, carry):
            pair = lax.rem(zed // 2 + step_of(m, NZ // 2), NZ // 2)
            coeffs = table[pl.ds(pl.multiple_of(pair * 128, 128), 128), :]
            out = dot(coeffs, buf_z[t].reshape(2 * KW, CH)).astype(BF16)
            buf_e[t, pl.ds(pair * 8, 8)] = out.reshape(8, WB, CH)

            def one(i, inner):
                send(3, t, buf_e, buf_u, True, 2 * pair + i // NY, turn(lax.rem(i, NY)))
                return inner

            return lax.fori_loop(0, 8, one, carry)

        lax.fori_loop(0, NZ // 2, chunk, 0)

    def modes(s, k):
        lanes = pl.ds(pl.multiple_of(k * BP, BP), BP)
        return jnp.concatenate([buf_s[s, :H, lanes], buf_s[s, H:, lanes]], axis=1)

    def put_modes(s, k, value):
        lanes = pl.ds(pl.multiple_of(k * BP, BP), BP)
        buf_o[s, :H, lanes] = value[:, :BP]
        buf_o[s, H:, lanes] = value[:, BP:]

    def mlp_forward(k, carry):
        pre = dot(modes(0, k), w1[...])
        squared = pre * pre
        tangent = jnp.tanh(GELU * (pre + 0.044715 * squared * pre))
        hidden = (0.5 * pre * (1.0 + tangent)).astype(BF16)
        buf_h[k] = hidden
        buf_slope[k] = 0.5 * (1.0 + tangent) + 0.5 * pre * (1.0 - tangent * tangent) * GELU * (
            1.0 + 3.0 * 0.044715 * squared
        )
        post = dot(hidden, w2[...])
        ratio = jnp.tanh(post / SHRINK)
        put_modes(0, k, (post - SHRINK * ratio).astype(BF16))
        weight = jnp.where(lat_me * KB + k == 0, 1.0, 2.0).astype(F32)
        buf_pass[k] = weight * (ratio * ratio)
        return carry

    g_first[...] = jnp.zeros_like(g_first)
    g_second[...] = jnp.zeros_like(g_second)

    def mlp_backward(k, carry):
        d_post = (modes(1, k).astype(F32) * buf_pass[k]).astype(BF16)
        d_pre = (dot_tb(d_post, w2[...]) * buf_slope[k]).astype(BF16)
        put_modes(1, k, dot_tb(d_pre, w1[...]).astype(BF16))
        g_second[...] += dot_ta(buf_h[k], d_post)
        g_first[...] += dot_ta(modes(0, k), d_pre)
        return carry

    def unpack(t, source, target):
        def body(y, carry):
            blocks = [buf_u[t, z * NY + y] for z in range(NZ)]
            for r in range(RH):
                pieces = [block[:, r * BS : (r + 1) * BS] for block in blocks]
                sums = jnp.concatenate(pieces, axis=1).astype(F32)
                at = y * RB + (t % 2) * RH + r
                target[at] = (source[at].astype(F32) + sums).astype(BF16)
            return carry

        lax.fori_loop(0, NY, body, 0)

    def fold():
        for which, total in ((0, g_first), (1, g_second)):
            real = total[:BS, :BP] + total[BP : BP + BS, BP:]
            imag = total[:BS, BP:] - total[BP : BP + BS, :BP]
            for ri, plane in ((0, real), (1, imag)):
                part_g[4 * which + 2 * ri] = plane[:GR]
                part_g[4 * which + 2 * ri + 1] = plane[GR:]

    def gather(stage, count, source_of, dst, target_of):
        def one(i, carry):
            source, target = target_of(i)
            pltpu.make_async_remote_copy(
                src_ref=source,
                dst_ref=dst,
                send_sem=g_send.at[stage],
                recv_sem=g_recv.at[stage],
                device_id=target,
                device_id_type=MESH,
            ).start()
            return carry

        lax.fori_loop(1, count, one, 0)
        if source_of is not None:
            pltpu.make_async_copy(source_of, dst, g_recv.at[stage]).start()

    def g_arrived(stage, ref):
        pltpu.make_async_copy(ref, ref, g_recv.at[stage]).wait()

    def g_left(stage, ref):
        pltpu.make_async_copy(ref, ref, g_send.at[stage]).wait()

    def to_lat(i):
        other = lax.rem(lat + i, NL)
        return part_g.at[other], (other, zed, why)

    def to_y(i):
        return part_p, (lat, zed, lax.rem(why + i, NY))

    def to_z(i):
        return part_q, (lat, lax.rem(zed + i, NZ), why)

    def to_x(i):
        return part_z, (2 * lax.rem(row + i, NL // 2) + core, zed, why)

    def grads_lat():
        fold()
        gather(0, NL, part_g.at[lat], part_l.at[lat], to_lat)

    def grads_y():
        g_arrived(0, part_l)
        total = part_l[0]
        for i in range(1, NL):
            total = total + part_l[i]
        part_p[...] = total
        gather(1, NY, part_p, part_y.at[why], to_y)

    def grads_z():
        g_arrived(1, part_y)
        total = part_y[0]
        for i in range(1, NY):
            total = total + part_y[i]
        part_q[...] = total * (1.0 / math.sqrt(H * KW))
        gather(2, NZ, part_q, part_z.at[zed], to_z)

    def grads_x():
        g_arrived(2, part_z)
        gather(3, NL // 2, part_z, part_c.at[core, row], to_x)

    def mate_copy():
        return pltpu.make_async_remote_copy(
            src_ref=part_c.at[core],
            dst_ref=part_c.at[core],
            send_sem=g_send.at[4],
            recv_sem=g_recv.at[4],
            device_id=(2 * row + 1 - core, zed, why),
            device_id_type=MESH,
        )

    def grads_core():
        g_arrived(3, part_c.at[core])
        mate_copy().start()

    def grads_out():
        g_arrived(4, part_c.at[0])
        for piece in range(NL):
            target = (out_first, out_second)[piece // 4]
            rows = slice((piece % 2) * GR, (piece % 2 + 1) * GR)
            for z in range(NZ):
                target[(piece // 2) % 2, z, rows, :] = part_c[piece % 2, piece // 2, z][:, :BS]
        g_left(0, part_g.at[pl.ds(0, NL - 1)])
        g_left(1, part_y.at[pl.ds(0, NY - 1)])
        g_left(2, part_z.at[pl.ds(0, NZ - 1)])
        g_left(3, part_c.at[0, pl.ds(0, NL // 2 - 1)])
        g_left(4, part_c.at[0])

    loads[0].wait()
    pack(0, feat)
    pl.semaphore_wait(barrier, 2 * NP - NY - 1)
    send_rows(0)
    pack(1, feat)
    send_rows(1)
    loads[1].wait()
    pack(2, cot)
    send_rows(2)
    pack(3, cot)
    send_rows(3)

    for source, target in ((wf, w1), (ws, w2)):
        target[...] = jnp.zeros_like(target)
        real = source[0, zed]
        imag = source[1, zed]
        target[0:BS, 0:BS] = real
        target[0:BS, BP : BP + BS] = imag
        target[BP : BP + BS, 0:BS] = -imag
        target[BP : BP + BS, BP : BP + BS] = real
    for load in loads[2:]:
        load.wait()

    for t in (0, 1):
        arrived(0, t, buf_x)
        lon_forward(t)
    for t in (0, 1):
        arrived(1, t, buf_r)
    lat_forward(0)
    lax.fori_loop(0, KB, mlp_forward, 0)
    lat_inverse(0)
    lat_inverse(1)
    for t in (2, 3):
        arrived(0, t, buf_x)
        lon_forward(t)
    for t in (0, 1):
        arrived(2, t, buf_z)
        lon_inverse(t)
    for t in (2, 3):
        arrived(1, t, buf_r)
    lat_forward(1)
    lax.fori_loop(0, KB, mlp_backward, 0)
    grads_lat()
    lat_inverse(2)
    lat_inverse(3)
    grads_y()
    grads_z()
    for t in (2, 3):
        arrived(2, t, buf_z)
        lon_inverse(t)
    grads_x()
    for t in (0, 1):
        arrived(3, t, buf_u)
        unpack(t, feat, mixed)
    grads_core()
    grads_out()
    for t in (2, 3):
        arrived(3, t, buf_u)
        unpack(t, cot, fgrad)
    for t in range(4):
        left(0, t, buf_a)
        left(1, t, buf_b)
        left(2, t, buf_d)
        left(3, t, buf_e)


def shards(features, cotangent, weight_first, weight_second):
    vmem = pl.BlockSpec(memory_space=pltpu.VMEM)
    hbm = pl.BlockSpec(memory_space=pltpu.HBM)
    chunks = (4, NP, WB, CH)
    flat = (4, NP, 8, CB)
    grads = jax.ShapeDtypeStruct((2, NB, BS, BS), F32)
    rows = jax.ShapeDtypeStruct(features.shape, BF16)
    piece = (GR, BP)
    return pl.pallas_call(
        kernel,
        out_shape=(rows, rows, grads, grads),
        in_specs=[hbm, hbm, vmem, vmem, hbm],
        out_specs=[vmem] * 4,
        scratch_shapes=[
            pltpu.VMEM(features.shape, BF16),
            pltpu.VMEM(features.shape, BF16),
        ]
        + [pltpu.VMEM((512, 512), BF16)] * 6
        + [
            pltpu.VMEM((2 * BP, 2 * BP), F32),
            pltpu.VMEM((2 * BP, 2 * BP), F32),
            pltpu.VMEM(chunks, BF16),
            pltpu.VMEM(chunks, BF16),
            pltpu.VMEM((1024, BP), F32),
            pltpu.VMEM(flat, BF16),
            pltpu.VMEM(flat, BF16),
            pltpu.VMEM((2, 2 * H, KB * BP), BF16),
            pltpu.VMEM((2, 2 * H, KB * BP), BF16),
            pltpu.VMEM((KB, 2 * BP, 2 * BP), BF16),
            pltpu.VMEM((KB, 2 * BP, 2 * BP), F32),
            pltpu.VMEM((KB, 2 * BP, 2 * BP), F32),
            pltpu.VMEM(chunks, BF16),
            pltpu.VMEM(chunks, BF16),
            pltpu.VMEM(chunks, BF16),
            pltpu.VMEM(chunks, BF16),
            pltpu.VMEM((2 * BP, 2 * BP), BF16),
            pltpu.VMEM((2 * BP, 2 * BP), BF16),
            pltpu.SemaphoreType.DMA((4, 4)),
            pltpu.SemaphoreType.DMA((4, 4)),
            pltpu.VMEM((NL,) + piece, F32),
            pltpu.VMEM((NL,) + piece, F32),
            pltpu.VMEM(piece, F32),
            pltpu.VMEM((NY,) + piece, F32),
            pltpu.VMEM(piece, F32),
            pltpu.VMEM((NZ,) + piece, F32),
            pltpu.VMEM((2, NL // 2, NZ) + piece, F32),
            pltpu.SemaphoreType.DMA((5,)),
            pltpu.SemaphoreType.DMA((5,)),
            pltpu.SemaphoreType.DMA((7,)),
        ],
        compiler_params=pltpu.CompilerParams(
            collective_id=0, has_side_effects=True, vmem_limit_bytes=58 << 20
        ),
    )(features, cotangent, weight_first, weight_second, jnp.asarray(tables()))


def solution(mesh):
    split = Mesh(mesh.devices.reshape(NL, NZ, NY), ("lat", "z", "y"))
    spec = P("lat", ("z", "y"), None)
    return jax.shard_map(
        shards,
        mesh=split,
        in_specs=(spec, spec, P(), P()),
        out_specs=(spec, spec, P(), P()),
        check_vma=False,
    )
```

```python
import math

import jax
import jax.numpy as jnp
import ml_dtypes
import numpy as np
from jax import lax
from jax.experimental import pallas as pl
from jax.experimental.pallas import tpu as pltpu
from jax.sharding import Mesh
from jax.sharding import PartitionSpec as P

NB = 8
BS = 96
BP = 128
NL, NZ, NY = 8, 8, 4
RB = 8
KB = 8
WB = 16
W = 512
H = 256
KW = 256
RH = 4
CH = RH * BS
CB = RB * BS
NP = 32
GR = 48
SHRINK = 0.01
GELU = 0.7978845608028654
CUBIC = 0.044715
MESH = pl.DeviceIdType.MESH
F32 = jnp.float32
BF16 = jnp.bfloat16


def wave_table(first, second, length):
    product = (first[:, None] * second[None, :]) % length
    angle = np.float32(2.0 * math.pi / length) * product.astype(np.float32)
    root = np.float32(math.sqrt(length))
    return (
        (np.cos(angle) / root).astype(ml_dtypes.bfloat16).astype(np.float32),
        (np.sin(angle) / root).astype(ml_dtypes.bfloat16).astype(np.float32),
    )


def tables():
    lon_cos, lon_sin = wave_table(np.arange(KW), np.arange(W), W)
    lon = np.stack([lon_cos.reshape(NP, KB, W), -lon_sin.reshape(NP, KB, W)], axis=1)
    lon = lon.reshape(2 * KW, W)
    doubled = np.full((NP, 2, KB), 2.0, np.float32)
    doubled[0, :, 0] = 1.0
    plain = lon.T
    scaled = plain * doubled.reshape(1, 2 * KW)
    lat_cos, lat_sin = wave_table(np.arange(H), np.arange(H), H)
    cos = lat_cos.reshape(H, NP, 2, RH).swapaxes(1, 2)
    sin = lat_sin.reshape(H, NP, 2, RH).swapaxes(1, 2)
    top = np.stack([cos, sin], axis=3)
    low = np.stack([-sin, cos], axis=3)
    lat = np.concatenate([top, low]).reshape(2 * H, 2 * H)
    return np.stack([lon, lat, lat.T, scaled, plain]).astype(ml_dtypes.bfloat16)


def dot(a, b):
    return jnp.dot(a, b, preferred_element_type=F32)


def dot_tb(a, b):
    return lax.dot_general(a, b, (((1,), (1,)), ((), ())), preferred_element_type=F32)


def dot_ta(a, b):
    return lax.dot_general(a, b, (((0,), (0,)), ((), ())), preferred_element_type=F32)


def step_of(index, size):
    half = (index + 1) // 2
    return lax.rem(half + (1 - lax.rem(index, 2)) * (size - 2 * half), size)


def kernel(
    feat_hbm, cot_hbm, wf, ws, h_tables,
    out_rows, out_grads,
    feat, cot, t_lon, t_lat, t_inv, t_scaled, t_plain, buf_w, g_first, g_second,
    buf_a, buf_x, buf_t, buf_b, buf_r, buf_s, buf_o, buf_h, buf_slope, buf_pass,
    buf_d, buf_z, buf_e, buf_u, w1, w2, send_sem, recv_sem,
    part_g, part_l, part_p, part_y, part_q, part_z, part_c, g_send, g_recv, load_sem, save_sem, ready,
):
    lat = lax.axis_index("lat")
    zed = lax.axis_index("z")
    why = lax.axis_index("y")
    lon_me = zed * NY + why
    lat_me = lat * NY + why

    loads = [
        pltpu.make_async_copy(source, target, load_sem.at[i])
        for i, (source, target) in enumerate(
            [
                (feat_hbm, feat), (cot_hbm, cot), (h_tables.at[0], t_lon), (h_tables.at[1], t_lat),
                (h_tables.at[2], t_inv), (h_tables.at[3], t_scaled), (h_tables.at[4], t_plain),
            ]
        )
    ]
    for load in loads:
        load.start()

    barrier = pltpu.get_barrier_semaphore()

    def greet(i, carry):
        z = lax.rem(zed + lax.rem(i, NZ), NZ)
        other = lax.rem(lat + i, NL)
        pl.semaphore_signal(barrier, inc=1, device_id=(lat, z, why), device_id_type=MESH)
        pl.semaphore_signal(barrier, inc=1, device_id=(other, zed, why), device_id_type=MESH)
        return carry

    def greet_y(semaphore):
        for i in range(1, NY):
            y = lax.rem(why + i, NY)
            pl.semaphore_signal(semaphore, inc=1, device_id=(lat, zed, y), device_id_type=MESH)

    greet_y(barrier)
    lax.fori_loop(1, NZ, greet, 0)

    def all_here():
        pl.semaphore_wait(barrier, NZ + NL + NY - 3)
        greet_y(ready)
        pl.semaphore_wait(ready, NY - 1)

    row = lat // 2
    core = lax.rem(lat, 2)

    def send(phase, t, src, dst, over_z, major, y):
        me = lon_me if over_z else lat_me
        to = major * NY + y
        target = (lat, major, y) if over_z else (major, zed, y)

        @pl.when(to != me)
        def _():
            pltpu.make_async_remote_copy(
                src_ref=src.at[t, to],
                dst_ref=dst.at[t, me],
                send_sem=send_sem.at[phase, t],
                recv_sem=recv_sem.at[phase, t],
                device_id=target,
                device_id_type=MESH,
            ).start()

        @pl.when(to == me)
        def _():
            pltpu.make_async_copy(src.at[t, me], dst.at[t, me], recv_sem.at[phase, t]).start()

    def turn(i):
        return lax.rem(why + i, NY)

    def arrived(phase, t, dst):
        pltpu.make_async_copy(dst.at[t], dst.at[t], recv_sem.at[phase, t]).wait()

    def left(phase, t, src):
        part = src.at[t, pl.ds(0, NP - 1)]
        pltpu.make_async_copy(part, part, send_sem.at[phase, t]).wait()

    def pack(t, source):
        def body(y, carry):
            rows = [source[y * RB + (t % 2) * RH + r] for r in range(RH)]
            for z in range(NZ):
                pieces = [r[:, z * BS : (z + 1) * BS] for r in rows]
                buf_a[t, z * NY + y] = jnp.concatenate(pieces, axis=1)
            return carry

        lax.fori_loop(0, NY, body, 0)

    def send_rows(t):
        def body(i, carry):
            z = lax.rem(zed + step_of(i // NY, NZ), NZ)
            send(0, t, buf_a, buf_x, True, z, turn(lax.rem(i, NY)))
            return carry

        lax.fori_loop(0, NP, body, 0)

    def widen(pair):
        zero = jnp.zeros((pair.shape[0], BP - BS), pair.dtype)
        return jnp.concatenate([pair[:, :BS], zero, pair[:, BS:], zero], axis=1)

    def lon_forward(t):
        for j in range(2):
            pair = buf_x[t, :, :, 2 * BS * j : 2 * BS * (j + 1)].reshape(W, 2 * BS)
            buf_w[:, 2 * BP * j : 2 * BP * (j + 1)] = widen(pair)
        view = buf_t.at[pl.ds(0, 512)].reshape(8, 2, RH, KB, BP)

        def chunk(m, carry):
            x = lax.rem(row + step_of(m, NL // 2), NL // 2)
            coeffs = t_lon[pl.ds(pl.multiple_of(x * 128, 128), 128), :]
            for j in range(2):
                out = dot(coeffs, buf_w[:, 2 * BP * j : 2 * BP * (j + 1)])
                view[:, :, 2 * j] = out[:, :BP].reshape(8, 2, KB, BP)
                view[:, :, 2 * j + 1] = out[:, BP:].reshape(8, 2, KB, BP)

            def one(i, inner):
                major = i // NY
                y = turn(lax.rem(i, NY))
                base = (major * NY + y) * 64
                pieces = [
                    buf_t[pl.ds(base + k, 8, stride=8), :].astype(BF16)[:, :BS] for k in range(KB)
                ]
                buf_b[t, 8 * x + major * NY + y] = jnp.concatenate(pieces, axis=1)
                send(1, t, buf_b, buf_r, False, 2 * x + major, y)
                return inner

            return lax.fori_loop(0, 8, one, carry)

        lax.fori_loop(0, NL // 2, chunk, 0)

    def lat_forward(s):
        for j in range(4):
            lanes = slice(2 * BS * j, 2 * BS * (j + 1))
            pair = jnp.concatenate(
                [buf_r[2 * s + h, :, :, lanes].reshape(H, 2 * BS) for h in range(2)], axis=0
            )
            out = dot(t_lat[...], widen(pair)).astype(BF16)
            buf_s[s, :, 2 * BP * j : 2 * BP * (j + 1)] = out

    def lat_inverse(t):
        view = buf_t.reshape(16, KB, 8, BP)

        def chunk(m, carry):
            half = lax.rem(row // 2 + m, 2)
            start = (t % 2) * H + half * 128
            coeffs = t_inv[pl.ds(pl.multiple_of(start, 128), 128), :]
            for j in range(4):
                out = dot(coeffs, buf_o[t // 2, :, 2 * BP * j : 2 * BP * (j + 1)])
                view[:, 2 * j] = out[:, :BP].reshape(16, 8, BP)
                view[:, 2 * j + 1] = out[:, BP:].reshape(16, 8, BP)

            def one(i, inner):
                major = i // NY
                y = turn(lax.rem(i, NY))
                base = (major * NY + y) * 64
                pieces = []
                for r in range(RH):
                    low = buf_t[pl.ds(base + r, 8, stride=8), :]
                    high = buf_t[pl.ds(base + RH + r, 8, stride=8), :]
                    pieces.append(jnp.concatenate([low, high], axis=0).astype(BF16)[:, :BS])
                buf_d[t, 16 * half + major * NY + y] = jnp.concatenate(pieces, axis=1)
                send(2, t, buf_d, buf_z, False, 4 * half + major, y)
                return inner

            return lax.fori_loop(0, 16, one, carry)

        lax.fori_loop(0, 2, chunk, 0)

    def lon_inverse(t):
        table = t_plain if t // 2 else t_scaled

        def chunk(m, carry):
            pair = lax.rem(zed // 2 + step_of(m, NZ // 2), NZ // 2)
            coeffs = table[pl.ds(pl.multiple_of(pair * 128, 128), 128), :]
            out = dot(coeffs, buf_z[t].reshape(2 * KW, CH)).astype(BF16)
            buf_e[t, pl.ds(pair * 8, 8)] = out.reshape(8, WB, CH)

            def one(i, inner):
                send(3, t, buf_e, buf_u, True, 2 * pair + i // NY, turn(lax.rem(i, NY)))
                return inner

            return lax.fori_loop(0, 8, one, carry)

        lax.fori_loop(0, NZ // 2, chunk, 0)

    def modes(s, k):
        lanes = pl.ds(pl.multiple_of(k * BP, BP), BP)
        return jnp.concatenate([buf_s[s, :H, lanes], buf_s[s, H:, lanes]], axis=1)

    def put_modes(s, k, value):
        lanes = pl.ds(pl.multiple_of(k * BP, BP), BP)
        buf_o[s, :H, lanes] = value[:, :BP]
        buf_o[s, H:, lanes] = value[:, BP:]

    def mlp_forward(k, carry):
        pre = dot(modes(0, k), w1[...])
        squared = pre * pre
        tangent = jnp.tanh(pre * (GELU + (GELU * CUBIC) * squared))
        gate = 0.5 + 0.5 * tangent
        active = pre * gate
        hidden = active.astype(BF16)
        buf_h[k] = hidden
        buf_slope[k] = gate + active * (1.0 - tangent) * (GELU + (3.0 * GELU * CUBIC) * squared)
        post = dot(hidden, w2[...])
        ratio = jnp.tanh(post * (1.0 / SHRINK))
        put_modes(0, k, (post - SHRINK * ratio).astype(BF16))
        weight = jnp.where(lat_me * KB + k == 0, 1.0, 2.0).astype(F32)
        buf_pass[k] = weight * (ratio * ratio)
        return carry

    g_first[...] = jnp.zeros_like(g_first)
    g_second[...] = jnp.zeros_like(g_second)

    def mlp_backward(k, carry):
        d_post = (modes(1, k).astype(F32) * buf_pass[k]).astype(BF16)
        d_pre = (dot_tb(d_post, w2[...]) * buf_slope[k]).astype(BF16)
        put_modes(1, k, dot_tb(d_pre, w1[...]).astype(BF16))
        g_second[...] += dot_ta(buf_h[k], d_post)
        g_first[...] += dot_ta(modes(0, k), d_pre)
        return carry

    saves = [
        pltpu.make_async_copy(buf_u.at[t], out_rows.at[t], save_sem.at[t]) for t in range(4)
    ] + [pltpu.make_async_copy(part_c, out_grads, save_sem.at[4])]

    def fold():
        for which, total in ((0, g_first), (1, g_second)):
            real = total[:BS, :BP] + total[BP : BP + BS, BP:]
            imag = total[:BS, BP:] - total[BP : BP + BS, :BP]
            for ri, plane in ((0, real), (1, imag)):
                part_g[4 * which + 2 * ri] = plane[:GR]
                part_g[4 * which + 2 * ri + 1] = plane[GR:]

    def gather(stage, count, source_of, dst, target_of):
        def one(i, carry):
            source, target = target_of(i)
            pltpu.make_async_remote_copy(
                src_ref=source,
                dst_ref=dst,
                send_sem=g_send.at[stage],
                recv_sem=g_recv.at[stage],
                device_id=target,
                device_id_type=MESH,
            ).start()
            return carry

        lax.fori_loop(1, count, one, 0)
        if source_of is not None:
            pltpu.make_async_copy(source_of, dst, g_recv.at[stage]).start()

    def g_arrived(stage, ref):
        pltpu.make_async_copy(ref, ref, g_recv.at[stage]).wait()

    def g_left(stage, ref):
        pltpu.make_async_copy(ref, ref, g_send.at[stage]).wait()

    def to_lat(i):
        other = lax.rem(lat + i, NL)
        return part_g.at[other], (other, zed, why)

    def to_y(i):
        return part_p, (lat, zed, lax.rem(why + i, NY))

    def to_z(i):
        return part_q, (lat, lax.rem(zed + i, NZ), why)

    def to_x(i):
        return part_z, (2 * lax.rem(row + i, NL // 2) + core, zed, why)

    def grads_lat():
        fold()
        gather(0, NL, part_g.at[lat], part_l.at[lat], to_lat)

    def grads_y():
        g_arrived(0, part_l)
        total = part_l[0]
        for i in range(1, NL):
            total = total + part_l[i]
        part_p[...] = total
        gather(1, NY, part_p, part_y.at[why], to_y)

    def grads_z():
        g_arrived(1, part_y)
        total = part_y[0]
        for i in range(1, NY):
            total = total + part_y[i]
        part_q[...] = (total * (1.0 / math.sqrt(H * KW))).astype(BF16)
        gather(2, NZ, part_q, part_z.at[zed], to_z)

    def grads_x():
        g_arrived(2, part_z)
        gather(3, NL // 2, part_z, part_c.at[core, row], to_x)

    def mate_copy():
        return pltpu.make_async_remote_copy(
            src_ref=part_c.at[core],
            dst_ref=part_c.at[core],
            send_sem=g_send.at[4],
            recv_sem=g_recv.at[4],
            device_id=(2 * row + 1 - core, zed, why),
            device_id_type=MESH,
        )

    def grads_core():
        g_arrived(3, part_c.at[core])
        mate_copy().start()

    def grads_out():
        g_arrived(4, part_c.at[0])
        saves[4].start()
        g_left(0, part_g.at[pl.ds(0, NL - 1)])
        g_left(1, part_y.at[pl.ds(0, NY - 1)])
        g_left(2, part_z.at[pl.ds(0, NZ - 1)])
        g_left(3, part_c.at[0, pl.ds(0, NL // 2 - 1)])
        g_left(4, part_c.at[0])

    loads[0].wait()
    pack(0, feat)
    all_here()
    send_rows(0)
    pack(1, feat)
    send_rows(1)
    loads[1].wait()
    pack(2, cot)
    send_rows(2)
    pack(3, cot)
    send_rows(3)

    for source, target in ((wf, w1), (ws, w2)):
        target[...] = jnp.zeros_like(target)
        real = source[0, zed]
        imag = source[1, zed]
        target[0:BS, 0:BS] = real
        target[0:BS, BP : BP + BS] = imag
        target[BP : BP + BS, 0:BS] = -imag
        target[BP : BP + BS, BP : BP + BS] = real
    for load in loads[2:]:
        load.wait()

    for t in (0, 1):
        arrived(0, t, buf_x)
        lon_forward(t)
    arrived(0, 2, buf_x)
    lon_forward(2)
    for t in (0, 1):
        arrived(1, t, buf_r)
    lat_forward(0)
    lax.fori_loop(0, KB, mlp_forward, 0)
    lat_inverse(0)
    lat_inverse(1)
    arrived(0, 3, buf_x)
    lon_forward(3)
    for t in (0, 1):
        arrived(2, t, buf_z)
        lon_inverse(t)
    for t in (2, 3):
        arrived(1, t, buf_r)
    lat_forward(1)
    lax.fori_loop(0, KB, mlp_backward, 0)
    grads_lat()
    lat_inverse(2)
    lat_inverse(3)
    grads_y()
    grads_z()
    for t in (2, 3):
        arrived(2, t, buf_z)
        lon_inverse(t)
    grads_x()
    for t in (0, 1):
        arrived(3, t, buf_u)
        saves[t].start()
    grads_core()
    grads_out()
    for t in (2, 3):
        arrived(3, t, buf_u)
        saves[t].start()
    for t in range(4):
        left(0, t, buf_a)
        left(1, t, buf_b)
        left(2, t, buf_d)
        left(3, t, buf_e)
    for save in saves:
        save.wait()


def finish_kernel(
    feat_hbm, cot_hbm, rows_hbm, grads_hbm, mixed_hbm, fgrad_hbm, first_hbm, second_hbm,
    feat, cot, rows, grads, mixed, fgrad, first, second, load_sem, save_sem, grad_sem,
):
    pairs = [(grads_hbm, grads)] + [(rows_hbm.at[t], rows.at[t]) for t in range(4)]
    pairs[1:1] = [(feat_hbm, feat)]
    pairs[4:4] = [(cot_hbm, cot)]
    loads = [
        pltpu.make_async_copy(source, target, load_sem.at[i])
        for i, (source, target) in enumerate(pairs)
    ]
    for load in loads:
        load.start()

    loads[0].wait()
    for piece in range(NL):
        target = (first, second)[piece // 4]
        into = slice((piece % 2) * GR, (piece % 2 + 1) * GR)
        for z in range(NZ):
            block = grads[piece % 2, piece // 2, z].astype(F32)
            target[(piece // 2) % 2, z, into, :] = block[:, :BS]
    grad_saves = [
        pltpu.make_async_copy(first, first_hbm, grad_sem.at[0]),
        pltpu.make_async_copy(second, second_hbm, grad_sem.at[1]),
    ]
    for save in grad_saves:
        save.start()

    for s, source, target, out in ((0, feat, mixed, mixed_hbm), (1, cot, fgrad, fgrad_hbm)):
        for load in loads[1 + 3 * s : 4 + 3 * s]:
            load.wait()

        def body(y, carry):
            for h in range(2):
                blocks = [rows[2 * s + h, z * NY + y] for z in range(NZ)]
                for r in range(RH):
                    pieces = [block[:, r * BS : (r + 1) * BS] for block in blocks]
                    sums = jnp.concatenate(pieces, axis=1).astype(F32)
                    at = y * RB + h * RH + r
                    target[at] = (source[at].astype(F32) + sums).astype(BF16)
            part = pl.ds(y * RB, RB)
            pltpu.make_async_copy(target.at[part], out.at[part], save_sem.at[s, y]).start()
            return carry

        lax.fori_loop(0, NY, body, 0)

    for save in grad_saves:
        save.wait()
    for s, target, out in ((0, mixed, mixed_hbm), (1, fgrad, fgrad_hbm)):
        for y in range(NY):
            part = pl.ds(y * RB, RB)
            pltpu.make_async_copy(target.at[part], out.at[part], save_sem.at[s, y]).wait()


def shards(features, cotangent, weight_first, weight_second):
    vmem = pl.BlockSpec(memory_space=pltpu.VMEM)
    hbm = pl.BlockSpec(memory_space=pltpu.HBM)
    chunks = (4, NP, WB, CH)
    flat = (4, NP, 8, CB)
    grads = jax.ShapeDtypeStruct((2, NB, BS, BS), F32)
    rows = jax.ShapeDtypeStruct(features.shape, BF16)
    piece = (GR, BP)
    gathered = (2, NL // 2, NZ) + piece
    out_rows, out_grads = pl.pallas_call(
        kernel,
        out_shape=(jax.ShapeDtypeStruct(chunks, BF16), jax.ShapeDtypeStruct(gathered, BF16)),
        in_specs=[hbm, hbm, vmem, vmem, hbm],
        out_specs=[hbm] * 2,
        scratch_shapes=[
            pltpu.VMEM(features.shape, BF16),
            pltpu.VMEM(features.shape, BF16),
        ]
        + [pltpu.VMEM((512, 512), BF16)] * 6
        + [
            pltpu.VMEM((2 * BP, 2 * BP), F32),
            pltpu.VMEM((2 * BP, 2 * BP), F32),
            pltpu.VMEM(chunks, BF16),
            pltpu.VMEM(chunks, BF16),
            pltpu.VMEM((1024, BP), F32),
            pltpu.VMEM(flat, BF16),
            pltpu.VMEM(flat, BF16),
            pltpu.VMEM((2, 2 * H, KB * BP), BF16),
            pltpu.VMEM((2, 2 * H, KB * BP), BF16),
            pltpu.VMEM((KB, 2 * BP, 2 * BP), BF16),
            pltpu.VMEM((KB, 2 * BP, 2 * BP), F32),
            pltpu.VMEM((KB, 2 * BP, 2 * BP), F32),
            pltpu.VMEM(chunks, BF16),
            pltpu.VMEM(chunks, BF16),
            pltpu.VMEM(chunks, BF16),
            pltpu.VMEM(chunks, BF16),
            pltpu.VMEM((2 * BP, 2 * BP), BF16),
            pltpu.VMEM((2 * BP, 2 * BP), BF16),
            pltpu.SemaphoreType.DMA((4, 4)),
            pltpu.SemaphoreType.DMA((4, 4)),
            pltpu.VMEM((NL,) + piece, F32),
            pltpu.VMEM((NL,) + piece, F32),
            pltpu.VMEM(piece, F32),
            pltpu.VMEM((NY,) + piece, F32),
            pltpu.VMEM(piece, BF16),
            pltpu.VMEM((NZ,) + piece, BF16),
            pltpu.VMEM((2, NL // 2, NZ) + piece, BF16),
            pltpu.SemaphoreType.DMA((5,)),
            pltpu.SemaphoreType.DMA((5,)),
            pltpu.SemaphoreType.DMA((7,)),
            pltpu.SemaphoreType.DMA((5,)),
            pltpu.SemaphoreType.REGULAR,
        ],
        compiler_params=pltpu.CompilerParams(
            collective_id=0, has_side_effects=True, vmem_limit_bytes=58 << 20
        ),
    )(features, cotangent, weight_first, weight_second, jnp.asarray(tables()))
    return pl.pallas_call(
        finish_kernel,
        out_shape=(rows, rows, grads, grads),
        in_specs=[hbm] * 4,
        out_specs=[hbm] * 4,
        scratch_shapes=[
            pltpu.VMEM(features.shape, BF16),
            pltpu.VMEM(features.shape, BF16),
            pltpu.VMEM(chunks, BF16),
            pltpu.VMEM(gathered, BF16),
            pltpu.VMEM(features.shape, BF16),
            pltpu.VMEM(features.shape, BF16),
            pltpu.VMEM((2, NB, BS, BS), F32),
            pltpu.VMEM((2, NB, BS, BS), F32),
            pltpu.SemaphoreType.DMA((7,)),
            pltpu.SemaphoreType.DMA((2, NY)),
            pltpu.SemaphoreType.DMA((2,)),
        ],
        compiler_params=pltpu.CompilerParams(vmem_limit_bytes=58 << 20),
    )(features, cotangent, out_rows, out_grads)


def solution(mesh):
    split = Mesh(mesh.devices.reshape(NL, NZ, NY), ("lat", "z", "y"))
    spec = P("lat", ("z", "y"), None)
    return jax.shard_map(
        shards,
        mesh=split,
        in_specs=(spec, spec, P(), P()),
        out_specs=(spec, spec, P(), P()),
        check_vma=False,
    )
```

```python
import math

import jax
import jax.numpy as jnp
import ml_dtypes
import numpy as np
from jax import lax
from jax.experimental import pallas as pl
from jax.experimental.pallas import tpu as pltpu
from jax.sharding import Mesh
from jax.sharding import PartitionSpec as P

NB = 8
BS = 96
BP = 128
NL, NZ, NY = 8, 8, 4
RB = 8
KB = 8
WB = 16
W = 512
H = 256
KW = 256
RH = 4
CH = RH * BS
CB = RB * BS
NP = 32
GR = 48
SHRINK = 0.01
GELU = 0.7978845608028654
CUBIC = 0.044715
MESH = pl.DeviceIdType.MESH
F32 = jnp.float32
BF16 = jnp.bfloat16


def wave_table(first, second, length):
    product = (first[:, None] * second[None, :]) % length
    angle = np.float32(2.0 * math.pi / length) * product.astype(np.float32)
    root = np.float32(math.sqrt(length))
    return (
        (np.cos(angle) / root).astype(ml_dtypes.bfloat16).astype(np.float32),
        (np.sin(angle) / root).astype(ml_dtypes.bfloat16).astype(np.float32),
    )


def tables():
    lon_cos, lon_sin = wave_table(np.arange(KW), np.arange(W), W)
    lon = np.stack([lon_cos.reshape(NP, KB, W), -lon_sin.reshape(NP, KB, W)], axis=1)
    lon = lon.reshape(2 * KW, W)
    doubled = np.full((NP, 2, KB), 2.0, np.float32)
    doubled[0, :, 0] = 1.0
    plain = lon.T
    scaled = plain * doubled.reshape(1, 2 * KW)
    lat_cos, lat_sin = wave_table(np.arange(H), np.arange(H), H)
    cos = lat_cos.reshape(H, NP, 2, RH).swapaxes(1, 2)
    sin = lat_sin.reshape(H, NP, 2, RH).swapaxes(1, 2)
    top = np.stack([cos, sin], axis=3)
    low = np.stack([-sin, cos], axis=3)
    lat = np.concatenate([top, low]).reshape(2 * H, 2 * H)
    return np.stack([lon, lat, lat.T, scaled, plain]).astype(ml_dtypes.bfloat16)


def dot(a, b):
    return jnp.dot(a, b, preferred_element_type=F32)


def dot_tb(a, b):
    return lax.dot_general(a, b, (((1,), (1,)), ((), ())), preferred_element_type=F32)


def dot_ta(a, b):
    return lax.dot_general(a, b, (((0,), (0,)), ((), ())), preferred_element_type=F32)


def step_of(index, size):
    half = (index + 1) // 2
    return lax.rem(half + (1 - lax.rem(index, 2)) * (size - 2 * half), size)


def kernel(
    feat_hbm, cot_hbm, wf, ws, h_tables,
    out_rows, out_grads,
    feat, cot, t_lon, t_lat, t_inv, t_scaled, t_plain, buf_w, g_first, g_second,
    buf_a, buf_x, buf_t, buf_b, buf_r, buf_s, buf_o, buf_h, buf_slope, buf_pass, buf_dq, buf_dp,
    buf_d, buf_z, buf_e, buf_u, w1, w2, send_sem, recv_sem,
    part_g, part_l, part_p, part_y, part_q, part_z, part_c, g_send, g_recv, load_sem, save_sem, ready,
):
    lat = lax.axis_index("lat")
    zed = lax.axis_index("z")
    why = lax.axis_index("y")
    lon_me = zed * NY + why
    lat_me = lat * NY + why

    loads = [
        pltpu.make_async_copy(source, target, load_sem.at[i])
        for i, (source, target) in enumerate(
            [
                (feat_hbm, feat), (cot_hbm, cot), (h_tables.at[0], t_lon), (h_tables.at[1], t_lat),
                (h_tables.at[2], t_inv), (h_tables.at[3], t_scaled), (h_tables.at[4], t_plain),
            ]
        )
    ]
    for load in loads:
        load.start()

    barrier = pltpu.get_barrier_semaphore()

    def greet(i, carry):
        z = lax.rem(zed + lax.rem(i, NZ), NZ)
        other = lax.rem(lat + i, NL)
        pl.semaphore_signal(barrier, inc=1, device_id=(lat, z, why), device_id_type=MESH)
        pl.semaphore_signal(barrier, inc=1, device_id=(other, zed, why), device_id_type=MESH)
        return carry

    def greet_y(semaphore):
        for i in range(1, NY):
            y = lax.rem(why + i, NY)
            pl.semaphore_signal(semaphore, inc=1, device_id=(lat, zed, y), device_id_type=MESH)

    greet_y(barrier)
    lax.fori_loop(1, NZ, greet, 0)

    def all_here():
        pl.semaphore_wait(barrier, NZ + NL + NY - 3)
        greet_y(ready)
        send_rows(0, (0,))
        pack(1, feat)
        pl.semaphore_wait(ready, NY - 1)

    row = lat // 2
    core = lax.rem(lat, 2)
    odd = lax.rem(zed, 2)

    def send(phase, t, src, dst, over_z, major, y, mine):
        me = lon_me if over_z else lat_me
        to = major * NY + y
        target = (lat, major, y) if over_z else (major, zed, y)

        def remote():
            pltpu.make_async_remote_copy(
                src_ref=src.at[t, to],
                dst_ref=dst.at[t, me],
                send_sem=send_sem.at[phase, t],
                recv_sem=recv_sem.at[phase, t],
                device_id=target,
                device_id_type=MESH,
            ).start()

        if mine is None:
            remote()
            return
        pl.when(jnp.logical_not(mine))(remote)

        @pl.when(mine)
        def _():
            pltpu.make_async_copy(src.at[t, me], dst.at[t, me], recv_sem.at[phase, t]).start()

    ys = [lax.rem(why + i, NY) for i in range(NY)]

    def arrived(phase, t, dst):
        pltpu.make_async_copy(dst.at[t], dst.at[t], recv_sem.at[phase, t]).wait()

    def left(phase, t, src):
        part = src.at[t, pl.ds(0, NP - 1)]
        pltpu.make_async_copy(part, part, send_sem.at[phase, t]).wait()

    def pack(t, source):
        def body(y, carry):
            rows = [source[y * RB + (t % 2) * RH + r] for r in range(RH)]
            for z in range(NZ):
                pieces = [r[:, z * BS : (z + 1) * BS] for r in rows]
                buf_a[t, z * NY + y] = jnp.concatenate(pieces, axis=1)
            return carry

        lax.fori_loop(0, NY, body, 0)

    def send_rows(t, turns=(0, 1, 2, 3)):
        def body(i, carry):
            z = lax.rem(zed + step_of(i, NZ), NZ)
            for j in turns:
                send(0, t, buf_a, buf_x, True, z, ys[j], None if j else i == 0)
            return carry

        lax.fori_loop(0, NZ, body, 0)

    def widen(pair):
        zero = jnp.zeros((pair.shape[0], BP - BS), pair.dtype)
        return jnp.concatenate([pair[:, :BS], zero, pair[:, BS:], zero], axis=1)

    def lon_forward(t):
        for j in range(2):
            pair = buf_x[t, :, :, 2 * BS * j : 2 * BS * (j + 1)].reshape(W, 2 * BS)
            buf_w[:, 2 * BP * j : 2 * BP * (j + 1)] = widen(pair)
        view = buf_t.at[pl.ds(0, 512)].reshape(8, 2, RH, KB, BP)

        def chunk(m, carry):
            x = lax.rem(row + step_of(m, NL // 2), NL // 2)
            coeffs = t_lon[pl.ds(pl.multiple_of(x * 128, 128), 128), :]
            for j in range(2):
                out = dot(coeffs, buf_w[:, 2 * BP * j : 2 * BP * (j + 1)])
                view[:, :, 2 * j] = out[:, :BP].reshape(8, 2, KB, BP)
                view[:, :, 2 * j + 1] = out[:, BP:].reshape(8, 2, KB, BP)

            for c in range(2):
                major = core if c == 0 else 1 - core
                for i, y in enumerate(ys):
                    base = (major * NY + y) * 64
                    pieces = [
                        buf_t[pl.ds(base + k, 8, stride=8), :].astype(BF16)[:, :BS]
                        for k in range(KB)
                    ]
                    buf_b[t, 8 * x + major * NY + y] = jnp.concatenate(pieces, axis=1)
                    mine = None if c or i else m == 0
                    send(1, t, buf_b, buf_r, False, 2 * x + major, y, mine)
            return carry

        lax.fori_loop(0, NL // 2, chunk, 0)

    def lat_forward(s):
        for j in range(4):
            lanes = slice(2 * BS * j, 2 * BS * (j + 1))
            pair = jnp.concatenate(
                [buf_r[2 * s + h, :, :, lanes].reshape(H, 2 * BS) for h in range(2)], axis=0
            )
            out = dot(t_lat[...], widen(pair)).astype(BF16)
            buf_s[s, :, 2 * BP * j : 2 * BP * (j + 1)] = out

    def lat_inverse(t):
        view = buf_t.reshape(16, KB, 8, BP)

        def chunk(m, carry):
            half = lax.rem(row // 2 + m, 2)
            start = (t % 2) * H + half * 128
            coeffs = t_inv[pl.ds(pl.multiple_of(start, 128), 128), :]
            for j in range(4):
                out = dot(coeffs, buf_o[t // 2, :, 2 * BP * j : 2 * BP * (j + 1)])
                view[:, 2 * j] = out[:, :BP].reshape(16, 8, BP)
                view[:, 2 * j + 1] = out[:, BP:].reshape(16, 8, BP)

            def one(a, inner):
                major = lax.rem(lat + a, 4)
                for i, y in enumerate(ys):
                    base = (major * NY + y) * 64
                    pieces = []
                    for r in range(RH):
                        low = buf_t[pl.ds(base + r, 8, stride=8), :]
                        high = buf_t[pl.ds(base + RH + r, 8, stride=8), :]
                        pieces.append(jnp.concatenate([low, high], axis=0).astype(BF16)[:, :BS])
                    buf_d[t, 16 * half + major * NY + y] = jnp.concatenate(pieces, axis=1)
                    mine = None if i else m + a == 0
                    send(2, t, buf_d, buf_z, False, 4 * half + major, y, mine)
                return inner

            return lax.fori_loop(0, 4, one, carry)

        lax.fori_loop(0, 2, chunk, 0)

    def lon_inverse(t):
        table = t_plain if t // 2 else t_scaled

        def chunk(m, carry):
            pair = lax.rem(zed // 2 + step_of(m, NZ // 2), NZ // 2)
            coeffs = table[pl.ds(pl.multiple_of(pair * 128, 128), 128), :]
            out = dot(coeffs, buf_z[t].reshape(2 * KW, CH)).astype(BF16)
            buf_e[t, pl.ds(pair * 8, 8)] = out.reshape(8, WB, CH)

            for c in range(2):
                major = 2 * pair + (odd if c == 0 else 1 - odd)
                for i, y in enumerate(ys):
                    mine = None if c or i else m == 0
                    send(3, t, buf_e, buf_u, True, major, y, mine)
            return carry

        lax.fori_loop(0, NZ // 2, chunk, 0)

    def modes(s, k):
        lanes = pl.ds(pl.multiple_of(k * BP, BP), BP)
        return jnp.concatenate([buf_s[s, :H, lanes], buf_s[s, H:, lanes]], axis=1)

    def put_modes(s, k, value):
        lanes = pl.ds(pl.multiple_of(k * BP, BP), BP)
        buf_o[s, :H, lanes] = value[:, :BP]
        buf_o[s, H:, lanes] = value[:, BP:]

    def mlp_forward(k, carry):
        pre = dot(modes(0, k), w1[...])
        squared = pre * pre
        tangent = jnp.tanh(pre * (GELU + (GELU * CUBIC) * squared))
        gate = 0.5 + 0.5 * tangent
        active = pre * gate
        hidden = active.astype(BF16)
        buf_h[k] = hidden
        buf_slope[k] = gate + active * (1.0 - tangent) * (GELU + (3.0 * GELU * CUBIC) * squared)
        post = dot(hidden, w2[...])
        ratio = jnp.tanh(post * (1.0 / SHRINK))
        put_modes(0, k, (post - SHRINK * ratio).astype(BF16))
        weight = jnp.where(lat_me * KB + k == 0, 1.0, 2.0).astype(F32)
        buf_pass[k] = weight * (ratio * ratio)
        return carry

    g_first[...] = jnp.zeros_like(g_first)
    g_second[...] = jnp.zeros_like(g_second)

    def mlp_backward(k, carry):
        d_post = (modes(1, k).astype(F32) * buf_pass[k]).astype(BF16)
        d_pre = (dot_tb(d_post, w2[...]) * buf_slope[k]).astype(BF16)
        put_modes(1, k, dot_tb(d_pre, w1[...]).astype(BF16))
        buf_dq[k] = d_post
        buf_dp[k] = d_pre
        return carry

    def mlp_grads(k, carry):
        g_second[...] += dot_ta(buf_h[k], buf_dq[k])
        g_first[...] += dot_ta(modes(0, k), buf_dp[k])
        return carry

    saves = [
        pltpu.make_async_copy(buf_u.at[t], out_rows.at[t], save_sem.at[t]) for t in range(4)
    ] + [pltpu.make_async_copy(part_c, out_grads, save_sem.at[4])]

    def fold():
        for which, total in ((0, g_first), (1, g_second)):
            real = total[:BS, :BP] + total[BP : BP + BS, BP:]
            imag = total[:BS, BP:] - total[BP : BP + BS, :BP]
            for ri, plane in ((0, real), (1, imag)):
                part_g[4 * which + 2 * ri] = plane[:GR]
                part_g[4 * which + 2 * ri + 1] = plane[GR:]

    def gather(stage, count, source_of, dst, target_of):
        def one(i, carry):
            source, target = target_of(i)
            pltpu.make_async_remote_copy(
                src_ref=source,
                dst_ref=dst,
                send_sem=g_send.at[stage],
                recv_sem=g_recv.at[stage],
                device_id=target,
                device_id_type=MESH,
            ).start()
            return carry

        lax.fori_loop(1, count, one, 0)
        if source_of is not None:
            pltpu.make_async_copy(source_of, dst, g_recv.at[stage]).start()

    def g_arrived(stage, ref):
        pltpu.make_async_copy(ref, ref, g_recv.at[stage]).wait()

    def g_left(stage, ref):
        pltpu.make_async_copy(ref, ref, g_send.at[stage]).wait()

    def to_lat(i):
        other = lax.rem(lat + i, NL)
        return part_g.at[other], (other, zed, why)

    def to_y(i):
        return part_p, (lat, zed, lax.rem(why + i, NY))

    def to_z(i):
        return part_q, (lat, lax.rem(zed + i, NZ), why)

    def to_x(i):
        return part_z, (2 * lax.rem(row + i, NL // 2) + core, zed, why)

    def grads_lat():
        fold()
        gather(0, NL, part_g.at[lat], part_l.at[lat], to_lat)

    def grads_y():
        g_arrived(0, part_l)
        total = part_l[0]
        for i in range(1, NL):
            total = total + part_l[i]
        part_p[...] = total
        gather(1, NY, part_p, part_y.at[why], to_y)

    def grads_z():
        g_arrived(1, part_y)
        total = part_y[0]
        for i in range(1, NY):
            total = total + part_y[i]
        part_q[...] = (total * (1.0 / math.sqrt(H * KW))).astype(BF16)
        gather(2, NZ, part_q, part_z.at[zed], to_z)

    def grads_x():
        g_arrived(2, part_z)
        gather(3, NL // 2, part_z, part_c.at[core, row], to_x)

    def mate_copy():
        return pltpu.make_async_remote_copy(
            src_ref=part_c.at[core],
            dst_ref=part_c.at[core],
            send_sem=g_send.at[4],
            recv_sem=g_recv.at[4],
            device_id=(2 * row + 1 - core, zed, why),
            device_id_type=MESH,
        )

    def grads_core():
        g_arrived(3, part_c.at[core])
        mate_copy().start()

    def grads_out():
        g_arrived(4, part_c.at[0])
        saves[4].start()
        g_left(0, part_g.at[pl.ds(0, NL - 1)])
        g_left(1, part_y.at[pl.ds(0, NY - 1)])
        g_left(2, part_z.at[pl.ds(0, NZ - 1)])
        g_left(3, part_c.at[0, pl.ds(0, NL // 2 - 1)])
        g_left(4, part_c.at[0])

    loads[0].wait()
    pack(0, feat)
    all_here()
    send_rows(0, (1, 2, 3))
    send_rows(1)
    loads[1].wait()
    pack(2, cot)
    send_rows(2)
    pack(3, cot)
    send_rows(3)

    for source, target in ((wf, w1), (ws, w2)):
        target[...] = jnp.zeros_like(target)
        real = source[0, zed]
        imag = source[1, zed]
        target[0:BS, 0:BS] = real
        target[0:BS, BP : BP + BS] = imag
        target[BP : BP + BS, 0:BS] = -imag
        target[BP : BP + BS, BP : BP + BS] = real
    for load in loads[2:]:
        load.wait()

    for t in (0, 1):
        arrived(0, t, buf_x)
        lon_forward(t)
    arrived(0, 2, buf_x)
    lon_forward(2)
    for t in (0, 1):
        arrived(1, t, buf_r)
    lat_forward(0)
    lax.fori_loop(0, KB, mlp_forward, 0, unroll=2)
    lat_inverse(0)
    lat_inverse(1)
    arrived(0, 3, buf_x)
    lon_forward(3)
    for t in (0, 1):
        arrived(2, t, buf_z)
        lon_inverse(t)
    for t in (2, 3):
        arrived(1, t, buf_r)
    lat_forward(1)
    lax.fori_loop(0, KB, mlp_backward, 0, unroll=2)
    lat_inverse(2)
    lat_inverse(3)
    lax.fori_loop(0, KB, mlp_grads, 0)
    grads_lat()
    arrived(2, 2, buf_z)
    lon_inverse(2)
    grads_y()
    grads_z()
    arrived(2, 3, buf_z)
    lon_inverse(3)
    grads_x()
    for t in (0, 1):
        arrived(3, t, buf_u)
        saves[t].start()
    grads_core()
    grads_out()
    for t in (2, 3):
        arrived(3, t, buf_u)
        saves[t].start()
    for t in range(4):
        left(0, t, buf_a)
        left(1, t, buf_b)
        left(2, t, buf_d)
        left(3, t, buf_e)
    for save in saves:
        save.wait()


def finish_kernel(
    feat_hbm, cot_hbm, rows_hbm, grads_hbm, mixed_hbm, fgrad_hbm, first_hbm, second_hbm,
    feat, cot, rows, grads, mixed, fgrad, first, second, load_sem, save_sem, grad_sem,
):
    pairs = [(grads_hbm, grads)] + [(rows_hbm.at[t], rows.at[t]) for t in range(4)]
    pairs[1:1] = [(feat_hbm, feat)]
    pairs[4:4] = [(cot_hbm, cot)]
    loads = [
        pltpu.make_async_copy(source, target, load_sem.at[i])
        for i, (source, target) in enumerate(pairs)
    ]
    for load in loads:
        load.start()

    loads[0].wait()
    for piece in range(NL):
        target = (first, second)[piece // 4]
        into = slice((piece % 2) * GR, (piece % 2 + 1) * GR)
        for z in range(NZ):
            block = grads[piece % 2, piece // 2, z].astype(F32)
            target[(piece // 2) % 2, z, into, :] = block[:, :BS]
    grad_saves = [
        pltpu.make_async_copy(first, first_hbm, grad_sem.at[0]),
        pltpu.make_async_copy(second, second_hbm, grad_sem.at[1]),
    ]
    for save in grad_saves:
        save.start()

    for s, source, target, out in ((0, feat, mixed, mixed_hbm), (1, cot, fgrad, fgrad_hbm)):
        for load in loads[1 + 3 * s : 4 + 3 * s]:
            load.wait()

        def body(y, carry):
            for h in range(2):
                blocks = [rows[2 * s + h, z * NY + y] for z in range(NZ)]
                for r in range(RH):
                    pieces = [block[:, r * BS : (r + 1) * BS] for block in blocks]
                    sums = jnp.concatenate(pieces, axis=1).astype(F32)
                    at = y * RB + h * RH + r
                    target[at] = (source[at].astype(F32) + sums).astype(BF16)
            part = pl.ds(y * RB, RB)
            pltpu.make_async_copy(target.at[part], out.at[part], save_sem.at[s, y]).start()
            return carry

        lax.fori_loop(0, NY, body, 0)

    for save in grad_saves:
        save.wait()
    for s, target, out in ((0, mixed, mixed_hbm), (1, fgrad, fgrad_hbm)):
        for y in range(NY):
            part = pl.ds(y * RB, RB)
            pltpu.make_async_copy(target.at[part], out.at[part], save_sem.at[s, y]).wait()


def shards(features, cotangent, weight_first, weight_second):
    vmem = pl.BlockSpec(memory_space=pltpu.VMEM)
    hbm = pl.BlockSpec(memory_space=pltpu.HBM)
    chunks = (4, NP, WB, CH)
    flat = (4, NP, 8, CB)
    grads = jax.ShapeDtypeStruct((2, NB, BS, BS), F32)
    rows = jax.ShapeDtypeStruct(features.shape, BF16)
    piece = (GR, BP)
    gathered = (2, NL // 2, NZ) + piece
    out_rows, out_grads = pl.pallas_call(
        kernel,
        out_shape=(jax.ShapeDtypeStruct(chunks, BF16), jax.ShapeDtypeStruct(gathered, BF16)),
        in_specs=[hbm, hbm, vmem, vmem, hbm],
        out_specs=[hbm] * 2,
        scratch_shapes=[
            pltpu.VMEM(features.shape, BF16),
            pltpu.VMEM(features.shape, BF16),
        ]
        + [pltpu.VMEM((512, 512), BF16)] * 6
        + [
            pltpu.VMEM((2 * BP, 2 * BP), F32),
            pltpu.VMEM((2 * BP, 2 * BP), F32),
            pltpu.VMEM(chunks, BF16),
            pltpu.VMEM(chunks, BF16),
            pltpu.VMEM((1024, BP), F32),
            pltpu.VMEM(flat, BF16),
            pltpu.VMEM(flat, BF16),
            pltpu.VMEM((2, 2 * H, KB * BP), BF16),
            pltpu.VMEM((2, 2 * H, KB * BP), BF16),
            pltpu.VMEM((KB, 2 * BP, 2 * BP), BF16),
            pltpu.VMEM((KB, 2 * BP, 2 * BP), F32),
            pltpu.VMEM((KB, 2 * BP, 2 * BP), F32),
            pltpu.VMEM((KB, 2 * BP, 2 * BP), BF16),
            pltpu.VMEM((KB, 2 * BP, 2 * BP), BF16),
            pltpu.VMEM(chunks, BF16),
            pltpu.VMEM(chunks, BF16),
            pltpu.VMEM(chunks, BF16),
            pltpu.VMEM(chunks, BF16),
            pltpu.VMEM((2 * BP, 2 * BP), BF16),
            pltpu.VMEM((2 * BP, 2 * BP), BF16),
            pltpu.SemaphoreType.DMA((4, 4)),
            pltpu.SemaphoreType.DMA((4, 4)),
            pltpu.VMEM((NL,) + piece, F32),
            pltpu.VMEM((NL,) + piece, F32),
            pltpu.VMEM(piece, F32),
            pltpu.VMEM((NY,) + piece, F32),
            pltpu.VMEM(piece, BF16),
            pltpu.VMEM((NZ,) + piece, BF16),
            pltpu.VMEM((2, NL // 2, NZ) + piece, BF16),
            pltpu.SemaphoreType.DMA((5,)),
            pltpu.SemaphoreType.DMA((5,)),
            pltpu.SemaphoreType.DMA((7,)),
            pltpu.SemaphoreType.DMA((5,)),
            pltpu.SemaphoreType.REGULAR,
        ],
        compiler_params=pltpu.CompilerParams(
            collective_id=0, has_side_effects=True, vmem_limit_bytes=58 << 20
        ),
    )(features, cotangent, weight_first, weight_second, jnp.asarray(tables()))
    return pl.pallas_call(
        finish_kernel,
        out_shape=(rows, rows, grads, grads),
        in_specs=[hbm] * 4,
        out_specs=[hbm] * 4,
        scratch_shapes=[
            pltpu.VMEM(features.shape, BF16),
            pltpu.VMEM(features.shape, BF16),
            pltpu.VMEM(chunks, BF16),
            pltpu.VMEM(gathered, BF16),
            pltpu.VMEM(features.shape, BF16),
            pltpu.VMEM(features.shape, BF16),
            pltpu.VMEM((2, NB, BS, BS), F32),
            pltpu.VMEM((2, NB, BS, BS), F32),
            pltpu.SemaphoreType.DMA((7,)),
            pltpu.SemaphoreType.DMA((2, NY)),
            pltpu.SemaphoreType.DMA((2,)),
        ],
        compiler_params=pltpu.CompilerParams(vmem_limit_bytes=58 << 20),
    )(features, cotangent, out_rows, out_grads)


def solution(mesh):
    split = Mesh(mesh.devices.reshape(NL, NZ, NY), ("lat", "z", "y"))
    spec = P("lat", ("z", "y"), None)
    return jax.shard_map(
        shards,
        mesh=split,
        in_specs=(spec, spec, P(), P()),
        out_specs=(spec, spec, P(), P()),
        check_vma=False,
    )
```

```python
import math

import jax
import jax.numpy as jnp
import ml_dtypes
import numpy as np
from jax import lax
from jax.experimental import pallas as pl
from jax.experimental.pallas import tpu as pltpu
from jax.sharding import Mesh
from jax.sharding import PartitionSpec as P

NB = 8
BS = 96
BP = 128
NL, NZ, NY = 8, 8, 4
RB = 8
KB = 8
WB = 16
W = 512
H = 256
KW = 256
RH = 4
CH = RH * BS
CB = RB * BS
NP = 32
GR = 48
SHRINK = 0.01
GELU = 0.7978845608028654
CUBIC = 0.044715
MESH = pl.DeviceIdType.MESH
F32 = jnp.float32
BF16 = jnp.bfloat16


def wave_table(first, second, length):
    product = (first[:, None] * second[None, :]) % length
    angle = np.float32(2.0 * math.pi / length) * product.astype(np.float32)
    root = np.float32(math.sqrt(length))
    return (
        (np.cos(angle) / root).astype(ml_dtypes.bfloat16).astype(np.float32),
        (np.sin(angle) / root).astype(ml_dtypes.bfloat16).astype(np.float32),
    )


def tables():
    lon_cos, lon_sin = wave_table(np.arange(KW), np.arange(W), W)
    lon = np.stack([lon_cos.reshape(NP, KB, W), -lon_sin.reshape(NP, KB, W)], axis=1)
    lon = lon.reshape(2 * KW, W)
    doubled = np.full((NP, 2, KB), 2.0, np.float32)
    doubled[0, :, 0] = 1.0
    plain = lon.T
    scaled = plain * doubled.reshape(1, 2 * KW)
    lat_cos, lat_sin = wave_table(np.arange(H), np.arange(H), H)
    cos = lat_cos.reshape(H, NP, 2, RH).swapaxes(1, 2)
    sin = lat_sin.reshape(H, NP, 2, RH).swapaxes(1, 2)
    top = np.stack([cos, sin], axis=3)
    low = np.stack([-sin, cos], axis=3)
    lat = np.concatenate([top, low]).reshape(2 * H, 2 * H)
    return np.stack([lon, lat, lat.T, scaled, plain]).astype(ml_dtypes.bfloat16)


def dot(a, b):
    return jnp.dot(a, b, preferred_element_type=F32)


def dot_tb(a, b):
    return lax.dot_general(a, b, (((1,), (1,)), ((), ())), preferred_element_type=F32)


def dot_ta(a, b):
    return lax.dot_general(a, b, (((0,), (0,)), ((), ())), preferred_element_type=F32)


def step_of(index, size):
    half = (index + 1) // 2
    return lax.rem(half + (1 - lax.rem(index, 2)) * (size - 2 * half), size)


def kernel(
    feat_hbm, cot_hbm, wf, ws, h_tables,
    out_rows, out_grads,
    feat, cot, t_lon, t_lat, t_inv, t_scaled, t_plain, buf_w, g_first, g_second,
    buf_a, buf_x, buf_t, buf_b, buf_r, buf_s, buf_o, buf_h, buf_slope, buf_pass, buf_dq, buf_dp,
    buf_d, buf_z, buf_e, buf_u, w1, w2, send_sem, recv_sem,
    part_g, part_l, part_p, part_y, part_q, part_z, part_c, g_send, g_recv, load_sem, save_sem, ready,
):
    lat = lax.axis_index("lat")
    zed = lax.axis_index("z")
    why = lax.axis_index("y")
    lon_me = zed * NY + why
    lat_me = lat * NY + why

    loads = [
        pltpu.make_async_copy(source, target, load_sem.at[i])
        for i, (source, target) in enumerate(
            [
                (feat_hbm, feat), (cot_hbm, cot), (h_tables.at[0], t_lon), (h_tables.at[1], t_lat),
                (h_tables.at[2], t_inv), (h_tables.at[3], t_scaled), (h_tables.at[4], t_plain),
            ]
        )
    ]
    for load in loads:
        load.start()

    barrier = pltpu.get_barrier_semaphore()

    def greet(i, carry):
        z = lax.rem(zed + lax.rem(i, NZ), NZ)
        other = lax.rem(lat + i, NL)
        pl.semaphore_signal(barrier, inc=1, device_id=(lat, z, why), device_id_type=MESH)
        pl.semaphore_signal(barrier, inc=1, device_id=(other, zed, why), device_id_type=MESH)
        return carry

    def greet_y(semaphore):
        for i in range(1, NY):
            y = lax.rem(why + i, NY)
            pl.semaphore_signal(semaphore, inc=1, device_id=(lat, zed, y), device_id_type=MESH)

    greet_y(barrier)
    lax.fori_loop(1, NZ, greet, 0)

    def all_here():
        pl.semaphore_wait(barrier, NZ + NL + NY - 3)
        greet_y(ready)
        send_rows(0, (0,))
        pack(1, feat)
        pl.semaphore_wait(ready, NY - 1)

    row = lat // 2
    core = lax.rem(lat, 2)
    odd = lax.rem(zed, 2)

    def send(phase, t, src, dst, over_z, major, y, mine):
        me = lon_me if over_z else lat_me
        to = major * NY + y
        target = (lat, major, y) if over_z else (major, zed, y)

        def remote():
            pltpu.make_async_remote_copy(
                src_ref=src.at[t, to],
                dst_ref=dst.at[t, me],
                send_sem=send_sem.at[phase, t],
                recv_sem=recv_sem.at[phase, t],
                device_id=target,
                device_id_type=MESH,
            ).start()

        if mine is None:
            remote()
            return
        pl.when(jnp.logical_not(mine))(remote)

        @pl.when(mine)
        def _():
            pltpu.make_async_copy(src.at[t, me], dst.at[t, me], recv_sem.at[phase, t]).start()

    ys = [lax.rem(why + i, NY) for i in range(NY)]

    def arrived(phase, t, dst):
        pltpu.make_async_copy(dst.at[t], dst.at[t], recv_sem.at[phase, t]).wait()

    def left(phase, t, src):
        part = src.at[t, pl.ds(0, NP - 1)]
        pltpu.make_async_copy(part, part, send_sem.at[phase, t]).wait()

    def pack(t, source):
        def body(y, carry):
            rows = [source[y * RB + (t % 2) * RH + r] for r in range(RH)]
            for z in range(NZ):
                pieces = [r[:, z * BS : (z + 1) * BS] for r in rows]
                buf_a[t, z * NY + y] = jnp.concatenate(pieces, axis=1)
            return carry

        lax.fori_loop(0, NY, body, 0)

    def send_rows(t, turns=(0, 1, 2, 3)):
        def body(i, carry):
            z = lax.rem(zed + step_of(i, NZ), NZ)
            for j in turns:
                send(0, t, buf_a, buf_x, True, z, ys[j], None if j else i == 0)
            return carry

        lax.fori_loop(0, NZ, body, 0)

    def widen(pair):
        zero = jnp.zeros((pair.shape[0], BP - BS), pair.dtype)
        return jnp.concatenate([pair[:, :BS], zero, pair[:, BS:], zero], axis=1)

    def lon_forward(t):
        for j in range(2):
            pair = buf_x[t, :, :, 2 * BS * j : 2 * BS * (j + 1)].reshape(W, 2 * BS)
            buf_w[:, 2 * BP * j : 2 * BP * (j + 1)] = widen(pair)
        def chunk(mm, carry):
            for p in range(2):
                m = 2 * mm + p
                view = buf_t.at[pl.ds(512 * p, 512)].reshape(8, 2, RH, KB, BP)
                x = lax.rem(row + step_of(m, NL // 2), NL // 2)
                coeffs = t_lon[pl.ds(pl.multiple_of(x * 128, 128), 128), :]
                for j in range(2):
                    out = dot(coeffs, buf_w[:, 2 * BP * j : 2 * BP * (j + 1)])
                    view[:, :, 2 * j] = out[:, :BP].reshape(8, 2, KB, BP)
                    view[:, :, 2 * j + 1] = out[:, BP:].reshape(8, 2, KB, BP)
                for c in range(2):
                    major = core if c == 0 else 1 - core
                    for i, y in enumerate(ys):
                        base = 512 * p + (major * NY + y) * 64
                        pieces = [
                            buf_t[pl.ds(base + k, 8, stride=8), :].astype(BF16)[:, :BS]
                            for k in range(KB)
                        ]
                        buf_b[t, 8 * x + major * NY + y] = jnp.concatenate(pieces, axis=1)
                        mine = None if p or c or i else mm == 0
                        send(1, t, buf_b, buf_r, False, 2 * x + major, y, mine)
            return carry

        lax.fori_loop(0, NL // 4, chunk, 0)

    def lat_forward(s):
        for j in range(4):
            lanes = slice(2 * BS * j, 2 * BS * (j + 1))
            pair = jnp.concatenate(
                [buf_r[2 * s + h, :, :, lanes].reshape(H, 2 * BS) for h in range(2)], axis=0
            )
            out = dot(t_lat[...], widen(pair)).astype(BF16)
            buf_s[s, :, 2 * BP * j : 2 * BP * (j + 1)] = out

    def lat_inverse(t):
        view = buf_t.reshape(16, KB, 8, BP)

        def chunk(m, carry):
            half = lax.rem(row // 2 + m, 2)
            start = (t % 2) * H + half * 128
            coeffs = t_inv[pl.ds(pl.multiple_of(start, 128), 128), :]
            for j in range(4):
                out = dot(coeffs, buf_o[t // 2, :, 2 * BP * j : 2 * BP * (j + 1)])
                view[:, 2 * j] = out[:, :BP].reshape(16, 8, BP)
                view[:, 2 * j + 1] = out[:, BP:].reshape(16, 8, BP)

            def one(a, inner):
                major = lax.rem(lat + a, 4)
                for i, y in enumerate(ys):
                    base = (major * NY + y) * 64
                    pieces = []
                    for r in range(RH):
                        low = buf_t[pl.ds(base + r, 8, stride=8), :]
                        high = buf_t[pl.ds(base + RH + r, 8, stride=8), :]
                        pieces.append(jnp.concatenate([low, high], axis=0).astype(BF16)[:, :BS])
                    buf_d[t, 16 * half + major * NY + y] = jnp.concatenate(pieces, axis=1)
                    mine = None if i else m + a == 0
                    send(2, t, buf_d, buf_z, False, 4 * half + major, y, mine)
                return inner

            return lax.fori_loop(0, 4, one, carry)

        lax.fori_loop(0, 2, chunk, 0)

    def lon_inverse(t):
        table = t_plain if t // 2 else t_scaled

        def chunk(m, carry):
            pair = lax.rem(zed // 2 + step_of(m, NZ // 2), NZ // 2)
            coeffs = table[pl.ds(pl.multiple_of(pair * 128, 128), 128), :]
            out = dot(coeffs, buf_z[t].reshape(2 * KW, CH)).astype(BF16)
            buf_e[t, pl.ds(pair * 8, 8)] = out.reshape(8, WB, CH)

            for c in range(2):
                major = 2 * pair + (odd if c == 0 else 1 - odd)
                for i, y in enumerate(ys):
                    mine = None if c or i else m == 0
                    send(3, t, buf_e, buf_u, True, major, y, mine)
            return carry

        lax.fori_loop(0, NZ // 2, chunk, 0)

    def modes(s, k):
        lanes = pl.ds(pl.multiple_of(k * BP, BP), BP)
        return jnp.concatenate([buf_s[s, :H, lanes], buf_s[s, H:, lanes]], axis=1)

    def put_modes(s, k, value):
        lanes = pl.ds(pl.multiple_of(k * BP, BP), BP)
        buf_o[s, :H, lanes] = value[:, :BP]
        buf_o[s, H:, lanes] = value[:, BP:]

    def mlp_forward(k, carry):
        pre = dot(modes(0, k), w1[...])
        squared = pre * pre
        tangent = jnp.tanh(pre * (GELU + (GELU * CUBIC) * squared))
        gate = 0.5 + 0.5 * tangent
        active = pre * gate
        hidden = active.astype(BF16)
        buf_h[k] = hidden
        buf_slope[k] = gate + active * (1.0 - tangent) * (GELU + (3.0 * GELU * CUBIC) * squared)
        post = dot(hidden, w2[...])
        ratio = jnp.tanh(post * (1.0 / SHRINK))
        put_modes(0, k, (post - SHRINK * ratio).astype(BF16))
        weight = jnp.where(lat_me * KB + k == 0, 1.0, 2.0).astype(F32)
        buf_pass[k] = weight * (ratio * ratio)
        return carry

    g_first[...] = jnp.zeros_like(g_first)
    g_second[...] = jnp.zeros_like(g_second)

    def mlp_backward(k, carry):
        d_post = (modes(1, k).astype(F32) * buf_pass[k]).astype(BF16)
        d_pre = (dot_tb(d_post, w2[...]) * buf_slope[k]).astype(BF16)
        put_modes(1, k, dot_tb(d_pre, w1[...]).astype(BF16))
        buf_dq[k] = d_post
        buf_dp[k] = d_pre
        return carry

    def mlp_grads(k, carry):
        g_second[...] += dot_ta(buf_h[k], buf_dq[k])
        g_first[...] += dot_ta(modes(0, k), buf_dp[k])
        return carry

    saves = [
        pltpu.make_async_copy(buf_u.at[t], out_rows.at[t], save_sem.at[t]) for t in range(4)
    ] + [pltpu.make_async_copy(part_c, out_grads, save_sem.at[4])]

    def fold():
        for which, total in ((0, g_first), (1, g_second)):
            real = total[:BS, :BP] + total[BP : BP + BS, BP:]
            imag = total[:BS, BP:] - total[BP : BP + BS, :BP]
            for ri, plane in ((0, real), (1, imag)):
                part_g[4 * which + 2 * ri] = plane[:GR]
                part_g[4 * which + 2 * ri + 1] = plane[GR:]

    def gather(stage, count, source_of, dst, target_of):
        def one(i, carry):
            source, target = target_of(i)
            pltpu.make_async_remote_copy(
                src_ref=source,
                dst_ref=dst,
                send_sem=g_send.at[stage],
                recv_sem=g_recv.at[stage],
                device_id=target,
                device_id_type=MESH,
            ).start()
            return carry

        lax.fori_loop(1, count, one, 0)
        if source_of is not None:
            pltpu.make_async_copy(source_of, dst, g_recv.at[stage]).start()

    def g_arrived(stage, ref):
        pltpu.make_async_copy(ref, ref, g_recv.at[stage]).wait()

    def g_left(stage, ref):
        pltpu.make_async_copy(ref, ref, g_send.at[stage]).wait()

    def to_lat(i):
        other = lax.rem(lat + i, NL)
        return part_g.at[other], (other, zed, why)

    def to_y(i):
        return part_p, (lat, zed, lax.rem(why + i, NY))

    def to_z(i):
        return part_q, (lat, lax.rem(zed + i, NZ), why)

    def to_x(i):
        return part_z, (2 * lax.rem(row + i, NL // 2) + core, zed, why)

    def grads_lat():
        fold()
        gather(0, NL, part_g.at[lat], part_l.at[lat], to_lat)

    def grads_y():
        g_arrived(0, part_l)
        total = part_l[0]
        for i in range(1, NL):
            total = total + part_l[i]
        part_p[...] = total
        gather(1, NY, part_p, part_y.at[why], to_y)

    def grads_z():
        g_arrived(1, part_y)
        total = part_y[0]
        for i in range(1, NY):
            total = total + part_y[i]
        part_q[...] = (total * (1.0 / math.sqrt(H * KW))).astype(BF16)
        gather(2, NZ, part_q, part_z.at[zed], to_z)

    def grads_x():
        g_arrived(2, part_z)
        gather(3, NL // 2, part_z, part_c.at[core, row], to_x)

    def mate_copy():
        return pltpu.make_async_remote_copy(
            src_ref=part_c.at[core],
            dst_ref=part_c.at[core],
            send_sem=g_send.at[4],
            recv_sem=g_recv.at[4],
            device_id=(2 * row + 1 - core, zed, why),
            device_id_type=MESH,
        )

    def grads_core():
        g_arrived(3, part_c.at[core])
        mate_copy().start()

    def grads_out():
        g_arrived(4, part_c.at[0])
        saves[4].start()
        g_left(0, part_g.at[pl.ds(0, NL - 1)])
        g_left(1, part_y.at[pl.ds(0, NY - 1)])
        g_left(2, part_z.at[pl.ds(0, NZ - 1)])
        g_left(3, part_c.at[0, pl.ds(0, NL // 2 - 1)])
        g_left(4, part_c.at[0])

    loads[0].wait()
    pack(0, feat)
    all_here()
    send_rows(0, (1, 2, 3))
    send_rows(1)
    loads[1].wait()
    pack(2, cot)
    send_rows(2)
    pack(3, cot)
    send_rows(3)

    for source, target in ((wf, w1), (ws, w2)):
        target[...] = jnp.zeros_like(target)
        real = source[0, zed]
        imag = source[1, zed]
        target[0:BS, 0:BS] = real
        target[0:BS, BP : BP + BS] = imag
        target[BP : BP + BS, 0:BS] = -imag
        target[BP : BP + BS, BP : BP + BS] = real
    for load in loads[2:]:
        load.wait()

    for t in (0, 1):
        arrived(0, t, buf_x)
        lon_forward(t)
    arrived(0, 2, buf_x)
    lon_forward(2)
    for t in (0, 1):
        arrived(1, t, buf_r)
    lat_forward(0)
    lax.fori_loop(0, KB, mlp_forward, 0, unroll=2)
    lat_inverse(0)
    lat_inverse(1)
    arrived(0, 3, buf_x)
    lon_forward(3)
    for t in (0, 1):
        arrived(2, t, buf_z)
        lon_inverse(t)
    for t in (2, 3):
        arrived(1, t, buf_r)
    lat_forward(1)
    lax.fori_loop(0, KB, mlp_backward, 0, unroll=2)
    lat_inverse(2)
    lat_inverse(3)
    lax.fori_loop(0, KB, mlp_grads, 0)
    grads_lat()
    arrived(2, 2, buf_z)
    lon_inverse(2)
    grads_y()
    grads_z()
    arrived(2, 3, buf_z)
    lon_inverse(3)
    grads_x()
    for t in (0, 1):
        arrived(3, t, buf_u)
        saves[t].start()
    grads_core()
    grads_out()
    for t in (2, 3):
        arrived(3, t, buf_u)
        saves[t].start()
    for t in range(4):
        left(0, t, buf_a)
        left(1, t, buf_b)
        left(2, t, buf_d)
        left(3, t, buf_e)
    for save in saves:
        save.wait()


def finish_kernel(
    feat_hbm, cot_hbm, rows_hbm, grads_hbm, mixed_hbm, fgrad_hbm, first_hbm, second_hbm,
    feat, cot, rows, grads, mixed, fgrad, first, second, load_sem, save_sem, grad_sem,
):
    pairs = [(grads_hbm, grads)] + [(rows_hbm.at[t], rows.at[t]) for t in range(4)]
    pairs[1:1] = [(feat_hbm, feat)]
    pairs[4:4] = [(cot_hbm, cot)]
    loads = [
        pltpu.make_async_copy(source, target, load_sem.at[i])
        for i, (source, target) in enumerate(pairs)
    ]
    for load in loads:
        load.start()

    loads[0].wait()
    for piece in range(NL):
        target = (first, second)[piece // 4]
        into = slice((piece % 2) * GR, (piece % 2 + 1) * GR)
        for z in range(NZ):
            block = grads[piece % 2, piece // 2, z].astype(F32)
            target[(piece // 2) % 2, z, into, :] = block[:, :BS]
    grad_saves = [
        pltpu.make_async_copy(first, first_hbm, grad_sem.at[0]),
        pltpu.make_async_copy(second, second_hbm, grad_sem.at[1]),
    ]
    for save in grad_saves:
        save.start()

    for s, source, target, out in ((0, feat, mixed, mixed_hbm), (1, cot, fgrad, fgrad_hbm)):
        for load in loads[1 + 3 * s : 4 + 3 * s]:
            load.wait()

        def body(y, carry):
            for h in range(2):
                blocks = [rows[2 * s + h, z * NY + y] for z in range(NZ)]
                for r in range(RH):
                    pieces = [block[:, r * BS : (r + 1) * BS] for block in blocks]
                    sums = jnp.concatenate(pieces, axis=1).astype(F32)
                    at = y * RB + h * RH + r
                    target[at] = (source[at].astype(F32) + sums).astype(BF16)
            part = pl.ds(y * RB, RB)
            pltpu.make_async_copy(target.at[part], out.at[part], save_sem.at[s, y]).start()
            return carry

        lax.fori_loop(0, NY, body, 0)

    for save in grad_saves:
        save.wait()
    for s, target, out in ((0, mixed, mixed_hbm), (1, fgrad, fgrad_hbm)):
        for y in range(NY):
            part = pl.ds(y * RB, RB)
            pltpu.make_async_copy(target.at[part], out.at[part], save_sem.at[s, y]).wait()


def shards(features, cotangent, weight_first, weight_second):
    vmem = pl.BlockSpec(memory_space=pltpu.VMEM)
    hbm = pl.BlockSpec(memory_space=pltpu.HBM)
    chunks = (4, NP, WB, CH)
    flat = (4, NP, 8, CB)
    grads = jax.ShapeDtypeStruct((2, NB, BS, BS), F32)
    rows = jax.ShapeDtypeStruct(features.shape, BF16)
    piece = (GR, BP)
    gathered = (2, NL // 2, NZ) + piece
    out_rows, out_grads = pl.pallas_call(
        kernel,
        out_shape=(jax.ShapeDtypeStruct(chunks, BF16), jax.ShapeDtypeStruct(gathered, BF16)),
        in_specs=[hbm, hbm, vmem, vmem, hbm],
        out_specs=[hbm] * 2,
        scratch_shapes=[
            pltpu.VMEM(features.shape, BF16),
            pltpu.VMEM(features.shape, BF16),
        ]
        + [pltpu.VMEM((512, 512), BF16)] * 6
        + [
            pltpu.VMEM((2 * BP, 2 * BP), F32),
            pltpu.VMEM((2 * BP, 2 * BP), F32),
            pltpu.VMEM(chunks, BF16),
            pltpu.VMEM(chunks, BF16),
            pltpu.VMEM((1024, BP), F32),
            pltpu.VMEM(flat, BF16),
            pltpu.VMEM(flat, BF16),
            pltpu.VMEM((2, 2 * H, KB * BP), BF16),
            pltpu.VMEM((2, 2 * H, KB * BP), BF16),
            pltpu.VMEM((KB, 2 * BP, 2 * BP), BF16),
            pltpu.VMEM((KB, 2 * BP, 2 * BP), F32),
            pltpu.VMEM((KB, 2 * BP, 2 * BP), F32),
            pltpu.VMEM((KB, 2 * BP, 2 * BP), BF16),
            pltpu.VMEM((KB, 2 * BP, 2 * BP), BF16),
            pltpu.VMEM(chunks, BF16),
            pltpu.VMEM(chunks, BF16),
            pltpu.VMEM(chunks, BF16),
            pltpu.VMEM(chunks, BF16),
            pltpu.VMEM((2 * BP, 2 * BP), BF16),
            pltpu.VMEM((2 * BP, 2 * BP), BF16),
            pltpu.SemaphoreType.DMA((4, 4)),
            pltpu.SemaphoreType.DMA((4, 4)),
            pltpu.VMEM((NL,) + piece, F32),
            pltpu.VMEM((NL,) + piece, F32),
            pltpu.VMEM(piece, F32),
            pltpu.VMEM((NY,) + piece, F32),
            pltpu.VMEM(piece, BF16),
            pltpu.VMEM((NZ,) + piece, BF16),
            pltpu.VMEM((2, NL // 2, NZ) + piece, BF16),
            pltpu.SemaphoreType.DMA((5,)),
            pltpu.SemaphoreType.DMA((5,)),
            pltpu.SemaphoreType.DMA((7,)),
            pltpu.SemaphoreType.DMA((5,)),
            pltpu.SemaphoreType.REGULAR,
        ],
        compiler_params=pltpu.CompilerParams(
            collective_id=0, has_side_effects=True, vmem_limit_bytes=58 << 20
        ),
    )(features, cotangent, weight_first, weight_second, jnp.asarray(tables()))
    return pl.pallas_call(
        finish_kernel,
        out_shape=(rows, rows, grads, grads),
        in_specs=[hbm] * 4,
        out_specs=[hbm] * 4,
        scratch_shapes=[
            pltpu.VMEM(features.shape, BF16),
            pltpu.VMEM(features.shape, BF16),
            pltpu.VMEM(chunks, BF16),
            pltpu.VMEM(gathered, BF16),
            pltpu.VMEM(features.shape, BF16),
            pltpu.VMEM(features.shape, BF16),
            pltpu.VMEM((2, NB, BS, BS), F32),
            pltpu.VMEM((2, NB, BS, BS), F32),
            pltpu.SemaphoreType.DMA((7,)),
            pltpu.SemaphoreType.DMA((2, NY)),
            pltpu.SemaphoreType.DMA((2,)),
        ],
        compiler_params=pltpu.CompilerParams(vmem_limit_bytes=58 << 20),
    )(features, cotangent, out_rows, out_grads)


def solution(mesh):
    split = Mesh(mesh.devices.reshape(NL, NZ, NY), ("lat", "z", "y"))
    spec = P("lat", ("z", "y"), None)
    return jax.shard_map(
        shards,
        mesh=split,
        in_specs=(spec, spec, P(), P()),
        out_specs=(spec, spec, P(), P()),
        check_vma=False,
    )
```
